256 devices in a mesh: req: 16 (over y, z_lo), kvh: 8 (over z_hi, x), ffn: 2 (over core).
Axes of the slice: x: 4, y: 4, z: 8 (z_hi: 2, z_lo: 4; z = z_hi * 4 + z_lo), core: 2. Of those that a mesh axis runs over, the one named last changes fastest.
Arguments:
- queries: bfloat16 [16, 64, 8192], P('req', None, 'kvh'), may hold values from -8 to 8
- tree_keys: bfloat16 [16, 64, 1024], P('req', None, 'kvh'), may hold values from -4.5 to 4.5
- tree_token_values: bfloat16 [16, 64, 1024], P('req', None, 'kvh'), may hold values from -6 to 6
- cache_keys: bfloat16 [16, 8, 8192, 128], P('req', 'kvh', 'ffn'), may hold values from -4.5 to 4.5
- cached_value_rows: bfloat16 [16, 8, 8192, 128], P('req', 'kvh', 'ffn'), may hold values from -6 to 6
- lengths: int32 [16], replicated, may hold values from 1 to 8192, 32768 in all
- parents: int32 [16, 64], P('req'), may hold values from 0 to 63, as said below
- residual: float32 [1024, 8192], P(('req', 'ffn'), 'kvh'), may hold values from -6 to 6
- out_weight: bfloat16 [8192, 8192], P('kvh', ('req', 'ffn')), may hold values from -0.0625 to 0.0625
- norm_gain: float32 [8192], P('kvh'), may hold values from 0.25 to 1.75
- gate_weight: bfloat16 [8192, 28672], P('kvh', ('req', 'ffn')), may hold values from -0.0625 to 0.0625
- up_weight: bfloat16 [8192, 28672], P('kvh', ('req', 'ffn')), may hold values from -0.0625 to 0.0625
- down_weight: bfloat16 [28672, 8192], P(('req', 'ffn'), 'kvh'), may hold values from -0.03125 to 0.03125
Outputs:
- layer_output: float32 [1024, 8192], P(('req', 'ffn'), 'kvh')
The draws below stay inside these ranges and needn't reach their ends.
Inputs may be any that keep to these rules, and one draw needn't show every extreme that they name: parents[r, 0] = 0, and parents[r, i] < i for every node i > 0. The lengths of all requests sum to 32768, and the largest is exactly 8192.
All inputs are finite; a program needn't handle non-finite values.
Results may differ from the reference program's by a relative error of at most 0.003.
Values may be sent and summed in bfloat16 or wider, within the bound.
No kernel may reach another device: no remote copies, remote signals or barrier semaphores. Data moves between devices by JAX's collectives and lax.ppermute only.
A program may use at most 64 MiB of HBM per device.

```python
import math
import jax
import jax.numpy as jnp
import numpy as np
from jax import lax

D = 8192
FF = 28672
QUERY_HEADS = 64
KEY_VALUE_HEADS = 8
HEAD_DIMENSION = 128
TREE_NODES = 64
CACHE_SLOTS = 8192
REQUEST_COUNT = 16
TOKENS = 1024


def sign_layout(key):
    random_bits = jax.random.randint(jax.random.fold_in(key, 7771), (KEY_VALUE_HEADS, HEAD_DIMENSION), 0, 2)
    return (random_bits * 2 - 1).astype(jnp.float32)


def draw_queries(key, part):
    own_key = jax.random.fold_in(key, 101)
    complete_shape = (REQUEST_COUNT, TREE_NODES, QUERY_HEADS * HEAD_DIMENSION)
    background = jnp.clip(2.0 * jax.random.normal(own_key, complete_shape, jnp.float32), -8.0, 8.0)
    value_pattern = sign_layout(key)
    spread_layout = jnp.repeat(value_pattern, QUERY_HEADS // KEY_VALUE_HEADS, axis=0).reshape(QUERY_HEADS * HEAD_DIMENSION)
    node_ids = jnp.arange(TREE_NODES)
    period = TREE_NODES // 4
    aligned = node_ids % period == TREE_NODES // 8
    strength = 5.6 + (node_ids // period % 3).astype(jnp.float32)
    inserted_entries = strength[:, None] * spread_layout[None, :]
    return jnp.where(aligned[None, :, None], inserted_entries[None], background).astype(jnp.bfloat16)


def draw_cache_keys(key, part):
    own_key = jax.random.fold_in(key, 202)
    complete_shape = (REQUEST_COUNT, KEY_VALUE_HEADS, CACHE_SLOTS, HEAD_DIMENSION)
    background = jnp.clip(jax.random.normal(own_key, complete_shape, jnp.float32), -4.5, 4.5)
    inserted_entries = 4.36 * sign_layout(key)[None, :, None, :]
    first_slot = (jnp.arange(CACHE_SLOTS) == 0)[None, None, :, None]
    return jnp.where(first_slot, inserted_entries, background).astype(jnp.bfloat16)


def draw_tree_keys(key, part):
    own_key = jax.random.fold_in(key, 303)
    complete_shape = (REQUEST_COUNT, TREE_NODES, KEY_VALUE_HEADS * HEAD_DIMENSION)
    background = jnp.clip(jax.random.normal(own_key, complete_shape, jnp.float32), -4.5, 4.5)
    inserted_entries = 4.4 * sign_layout(key).reshape(KEY_VALUE_HEADS * HEAD_DIMENSION)
    root_node = (jnp.arange(TREE_NODES) == 0)[None, :, None]
    return jnp.where(root_node, inserted_entries[None, None, :], background).astype(jnp.bfloat16)


def draw_parents(key, part):
    own_key = jax.random.fold_in(key, 404)
    draws = jax.random.randint(own_key, (REQUEST_COUNT, TREE_NODES), 0, 1 << 20)
    node_ids = jnp.arange(TREE_NODES, dtype=jnp.int32)
    chosen = draws % jnp.maximum(node_ids, 1)[None, :]
    return jnp.where(node_ids[None, :] == 0, 0, chosen).astype(jnp.int32)


def level_of(rng, extent, pieces, low, largest):
    factor_of, own = 1.0, jax.random.fold_in(rng, 6)
    for axis_at, parts in pieces:
        heights = jnp.exp(jax.random.uniform(jax.random.fold_in(own, axis_at), (parts,), jnp.float32, low / len(pieces), largest / len(pieces)))
        factor_of = factor_of * jnp.repeat(heights, extent[axis_at] // parts).reshape([-1 if axis == axis_at else 1 for axis in range(len(extent))])
    return factor_of


def profile(amount, total, reach, slope):
    portions = [(1 << 20) // math.isqrt(standing ** slope) + 1 for standing in range(2, amount + 1)]
    rest, given = total - reach - (amount - 1), [1] * (amount - 1)
    while rest > 0:
        candidates = [i for i in range(amount - 1) if given[i] < reach]
        mass, remaining = sum([portions[i] for i in candidates]), rest
        for i in candidates:
            more = min(reach - given[i], max(1, remaining * portions[i] // mass), rest)
            given[i] = given[i] + more
            rest = rest - more
    return np.array([reach] + given)


def uneven_parts(key, number_of, total, reach, skew):
    if number_of == 2:
        one = jax.random.randint(key, (), max(1, total - reach), min(reach, total - 1) + 1)
        return jnp.stack([one, total - one])
    tallies = jnp.asarray(profile(number_of, total, reach, skew), jnp.int32)
    couples = (number_of - 1) // 2
    giver, taker = tallies[1:1 + 2 * couples:2], tallies[2:2 + 2 * couples:2]
    slack = jnp.minimum(giver - 1, reach - taker)
    moved = jax.random.randint(jax.random.fold_in(key, 1), (couples,), 0, 1 << 20) % (slack + 1)
    tallies = tallies.at[1:1 + 2 * couples:2].set(giver - moved).at[2:2 + 2 * couples:2].set(taker + moved)
    return tallies[jax.random.permutation(jax.random.fold_in(key, 2), number_of)]


def noise(rng, extent, scale, most, shards=(), held_as=jnp.bfloat16):
    factor_of = level_of(rng, extent, shards, -0.22, 0.18) if shards else 1.0
    result = jax.random.normal(rng, extent, jnp.float32) * scale * factor_of
    return jnp.minimum(jnp.maximum(result, -most), most).astype(held_as)


def setup_inputs(seed: int = 0) -> dict:
    seeds = jax.random.split(jax.random.key(seed), 14)
    queries = draw_queries(jax.random.fold_in(seeds[13], 71), 0)
    tree_keys = draw_tree_keys(jax.random.fold_in(seeds[13], 71), 0)
    tree_token_values = noise(seeds[2], (REQUEST_COUNT, TREE_NODES, KEY_VALUE_HEADS * HEAD_DIMENSION), 1.0, 6.0, ((0, 16), (2, 8)))
    cache_keys = draw_cache_keys(jax.random.fold_in(seeds[13], 71), 0)
    cached_value_rows = noise(seeds[4], (REQUEST_COUNT, KEY_VALUE_HEADS, CACHE_SLOTS, HEAD_DIMENSION), 1.0, 6.0, ((0, 16), (1, 8), (2, 2)))
    lengths = uneven_parts(seeds[5], REQUEST_COUNT, REQUEST_COUNT * CACHE_SLOTS // 4, CACHE_SLOTS, 2).astype(jnp.int32)
    parents = draw_parents(jax.random.fold_in(seeds[13], 71), 0)
    residual = noise(seeds[7], (TOKENS, D), 1.0, 6.0, ((0, 32), (1, 8)), jnp.float32)
    out_weight = noise(seeds[8], (QUERY_HEADS * HEAD_DIMENSION, D), (QUERY_HEADS * HEAD_DIMENSION) ** -0.5, 0.0625, ((0, 8), (1, 32)))
    norm_gain = jnp.clip(1.0 + 0.15 * jax.random.normal(seeds[9], (D,), jnp.float32), 0.25, 1.75)
    gate_weight = noise(seeds[10], (D, FF), D ** -0.5, 0.0625, ((0, 8), (1, 32)))
    up_weight = noise(seeds[11], (D, FF), D ** -0.5, 0.0625, ((0, 8), (1, 32)))
    down_weight = noise(seeds[12], (FF, D), FF ** -0.5, 0.03125, ((0, 32), (1, 8)))
    return dict(queries=queries, tree_keys=tree_keys, tree_token_values=tree_token_values, cache_keys=cache_keys, cached_value_rows=cached_value_rows, lengths=lengths, parents=parents, residual=residual, out_weight=out_weight, norm_gain=norm_gain, gate_weight=gate_weight, up_weight=up_weight, down_weight=down_weight)


MASKED = -1e+30
EPSILON = 1e-05

def ancestors(parent_row, node_total):
    node_ids = jnp.arange(node_total, dtype=jnp.int32)
    upward = (parent_row[:, None] == node_ids[None, :]).astype(jnp.float32)
    reachable = jnp.minimum(jnp.eye(node_total, dtype=jnp.float32) + upward, 1.0)
    for repeat_count in range((node_total - 1).bit_length()):
        reachable = jnp.minimum(jnp.dot(reachable, reachable, precision=lax.Precision.HIGHEST), 1.0)
    return reachable > 0.5

def attend_request(inputs):
    query_tile_rows, tree_key_rows, tree_value_block, keys_all, values_all, length, parent_row = inputs
    query_group_width = QUERY_HEADS // KEY_VALUE_HEADS
    score_scale = HEAD_DIMENSION ** (-0.5)
    query_complete = query_tile_rows.astype(jnp.float32).reshape(TREE_NODES, KEY_VALUE_HEADS, query_group_width, HEAD_DIMENSION)
    cache_scores = jnp.einsum('nhgd,hpd->hgnp', query_complete, keys_all.astype(jnp.float32)) * score_scale
    tree_complete = tree_key_rows.astype(jnp.float32).reshape(TREE_NODES, KEY_VALUE_HEADS, HEAD_DIMENSION)
    tree_score_matrix = jnp.einsum('czpk,izk->zpci', query_complete, tree_complete) * score_scale
    positions = jnp.arange(CACHE_SLOTS, dtype=jnp.int32)
    cache_usable = jnp.broadcast_to((positions < length)[None, None, None, :], cache_scores.shape)
    tree_usable = jnp.broadcast_to(ancestors(parent_row, TREE_NODES)[None, None], tree_score_matrix.shape)
    scores = jnp.concatenate([cache_scores, tree_score_matrix], axis=-1)
    usable = jnp.concatenate([cache_usable, tree_usable], axis=-1)
    scores = jnp.where(usable, scores, MASKED)
    highest = lax.optimization_barrier(jnp.max(scores, axis=-1, keepdims=True))
    weights = jnp.where(usable, jnp.exp(scores - highest), 0.0)
    total = lax.optimization_barrier(jnp.sum(weights, axis=-1))
    tree_value_rows = tree_value_block.astype(jnp.float32).reshape(TREE_NODES, KEY_VALUE_HEADS, HEAD_DIMENSION).transpose(1, 0, 2)
    values = jnp.concatenate([values_all.astype(jnp.float32), tree_value_rows], axis=1)
    mixed = jnp.einsum('hgnk,hkd->hgnd', weights, values, precision=lax.Precision.HIGHEST) / total[..., None]
    return mixed.transpose(2, 0, 1, 3).reshape(TREE_NODES, QUERY_HEADS * HEAD_DIMENSION).astype(jnp.bfloat16)

def reference(queries, tree_keys, tree_token_values, cache_keys, cached_value_rows, lengths, parents, residual, out_weight, norm_gain, gate_weight, up_weight, down_weight):
    attention = lax.map(attend_request, (queries, tree_keys, tree_token_values, cache_keys, cached_value_rows, lengths, parents))
    attention = attention.reshape(TOKENS, QUERY_HEADS * HEAD_DIMENSION)
    state = residual + jnp.dot(attention, out_weight, preferred_element_type=jnp.float32)
    mean_square = lax.optimization_barrier(jnp.mean(state * state, axis=1, keepdims=True))
    normed = (state * lax.rsqrt(mean_square + EPSILON) * norm_gain).astype(jnp.bfloat16)
    gate = jnp.dot(normed, gate_weight, preferred_element_type=jnp.float32)
    upward = jnp.dot(normed, up_weight, preferred_element_type=jnp.float32)
    activation = (jax.nn.silu(gate) * upward).astype(jnp.bfloat16)
    return state + jnp.dot(activation, down_weight, preferred_element_type=jnp.float32)
```

```python
import jax
import jax.numpy as jnp
from jax import lax
from jax.sharding import Mesh
from jax.sharding import PartitionSpec as P

KB = 512
REQ = ("y", "zl")
KVH = ("zh", "x")
GRID = ("y", "zl", "zh", "x")
SIZES = (4, 4, 2, 4)
MASKED = -1e30
EPSILON = 1e-05
MASKS = (0, 3, 1, 2)


def sent(array, target):
    pairs = []
    for source in range(128):
        x, zh, zl, y = source % 4, source // 4 % 2, source // 8 % 4, source // 32
        to = target(y, zl, zh, x)
        pairs.append((source, ((to[0] * 4 + to[1]) * 2 + to[2]) * 4 + to[3]))
    return lax.ppermute(array, GRID, pairs)


def over_x(array, mask):
    return lax.ppermute(array, "x", [(i, i ^ mask) for i in range(4)])


def over_zh(array):
    return lax.ppermute(array, "zh", [(0, 1), (1, 0)])


def over_core(array):
    return lax.ppermute(array, "core", [(0, 1), (1, 0)])


def line_target(place):
    part, step = divmod(place, 2)
    return lambda y, zl, zh, x: (y, zl ^ (2 * (part ^ zh) + step), zh, x)


def ring_target(mask):
    return lambda y, zl, zh, x: (y ^ x ^ mask, zl, zh, x)


def home_target(place):
    part, step = divmod(place, 2)
    return lambda y, zl, zh, x: (
        y ^ x,
        zl ^ (2 * (part ^ zh) + step),
        y >> 1,
        2 * (y & 1) + (zl >> 1),
    )


def gathered(rows):
    line = jnp.concatenate([sent(rows, line_target(place)) for place in range(4)])
    return {mask: sent(line, ring_target(mask)) for mask in MASKS}


def dot(a, b):
    return jnp.dot(a, b, preferred_element_type=jnp.float32)


def summed_over_x(blocks, first, second, dtype):
    pair = lambda a, b: jnp.concatenate([blocks[a], blocks[b]])
    away1, away2 = pair(1, 2), pair(3, 2)
    stay1, stay2 = pair(0, 3), pair(0, 1)
    half = blocks[0].shape[0]
    got1 = [over_x(dot(away1, w).astype(dtype), 1) for w in first]
    got2 = [over_x(dot(away2, w).astype(dtype), 3) for w in second]
    sum1 = [dot(stay1, w) + g for w, g in zip(first, got1)]
    sum2 = [dot(stay2, w) + g for w, g in zip(second, got2)]
    last1 = [s[:half] + over_x(s[half:].astype(dtype), 3) for s in sum1]
    last2 = [s[:half] + over_x(s[half:].astype(dtype), 1) for s in sum2]
    return last1, last2


def ancestors(parent_row, node_total):
    node_ids = jnp.arange(node_total, dtype=jnp.int32)
    upward = (parent_row[:, None] == node_ids[None, :]).astype(jnp.float32)
    reachable = jnp.minimum(jnp.eye(node_total, dtype=jnp.float32) + upward, 1.0)
    for repeat_count in range((node_total - 1).bit_length()):
        reachable = jnp.minimum(jnp.dot(reachable, reachable, precision=lax.Precision.HIGHEST), 1.0)
    return reachable > 0.5


def absorb(running, scores, usable, value_block):
    value_sum, row_max, row_total = running
    scores = jnp.where(usable, scores, MASKED)
    highest = jnp.maximum(row_max, jnp.max(scores, axis=-1))
    weights = jnp.where(usable, jnp.exp(scores - highest[..., None]), 0.0)
    factor = jnp.exp(row_max - highest)
    row_total = row_total * factor + jnp.sum(weights, axis=-1)
    value_sum = value_sum * factor[..., None] + jnp.einsum(
        "rk,kd->rd", weights, value_block.astype(jnp.float32), precision=lax.Precision.HIGHEST
    )
    return (value_sum, highest, row_total)


def combine(first, second):
    value_left, max_left, total_left = first
    value_right, max_right, total_right = second
    highest = jnp.maximum(max_left, max_right)
    factor_left = jnp.exp(max_left - highest)
    factor_right = jnp.exp(max_right - highest)
    value_sum = value_left * factor_left[..., None] + value_right * factor_right[..., None]
    return (value_sum, highest, total_left * factor_left + total_right * factor_right)


def attended(queries, tree_keys, tree_values, keys, values, length, parent_row, core):
    node_total, width = queries.shape
    half_len, head_size = keys.shape
    heads = width // head_size
    scale = head_size ** (-0.5)
    query_rows = queries.reshape(node_total, heads, head_size).transpose(1, 0, 2)
    query_rows = query_rows.reshape(heads * node_total, head_size)
    rows = heads * node_total
    running = (
        jnp.zeros((rows, head_size), jnp.float32),
        jnp.full((rows,), MASKED, jnp.float32),
        jnp.zeros((rows,), jnp.float32),
    )
    live_len = jnp.clip(length - core * half_len, 0, half_len)
    kb = min(KB, half_len)

    def visit(block_idx, running):
        begin_pos = block_idx * kb
        key_block = lax.dynamic_slice_in_dim(keys, begin_pos, kb, 0)
        value_block = lax.dynamic_slice_in_dim(values, begin_pos, kb, 0)
        positions = begin_pos + jnp.arange(kb, dtype=jnp.int32)
        usable = (positions < live_len)[None, :]
        scores = (
            jnp.einsum("rd,kd->rk", query_rows, key_block, preferred_element_type=jnp.float32)
            * scale
        )
        return absorb(running, scores, usable, value_block)

    running = lax.fori_loop(0, (live_len + kb - 1) // kb, visit, running)
    tree_usable = jnp.tile(ancestors(parent_row, node_total), (heads, 1)) & (core == 0)
    tree_scores = (
        jnp.einsum("rd,kd->rk", query_rows, tree_keys, preferred_element_type=jnp.float32) * scale
    )
    value_sum, row_max, row_total = absorb(running, tree_scores, tree_usable, tree_values)
    halves = (
        value_sum.reshape(heads, 2, node_total // 2, head_size),
        row_max.reshape(heads, 2, node_total // 2),
        row_total.reshape(heads, 2, node_total // 2),
    )
    own = [lax.dynamic_index_in_dim(part, core, 1, keepdims=False) for part in halves]
    other = [lax.dynamic_index_in_dim(part, 1 - core, 1, keepdims=False) for part in halves]
    numbers = over_core(jnp.stack(other[1:]))
    value_sum, row_max, row_total = combine(own, (over_core(other[0]), numbers[0], numbers[1]))
    attention = (value_sum / row_total[..., None]).astype(jnp.bfloat16)
    return attention.transpose(1, 0, 2).reshape(node_total // 2, width)


def local(
    queries,
    tree_keys,
    tree_token_values,
    cache_keys,
    cached_value_rows,
    lengths,
    parents,
    residual,
    out_weight,
    norm_gain,
    gate_weight,
    up_weight,
    down_weight,
):
    core = lax.axis_index("core")
    features = norm_gain.shape[0] * 8
    other_out = over_core(out_weight)
    other_gate = over_core(gate_weight)
    other_up = over_core(up_weight)
    other_down = over_core(down_weight)
    length = lax.dynamic_index_in_dim(lengths, lax.axis_index(REQ), keepdims=False)
    attention = attended(
        queries[0],
        tree_keys[0],
        tree_token_values[0],
        cache_keys[0, 0],
        cached_value_rows[0, 0],
        length,
        parents[0],
        core,
    )
    tokens = attention.shape[0]

    (mine,), (theirs,) = summed_over_x(
        gathered(attention), [out_weight], [other_out], jnp.float32
    )
    both = jnp.concatenate([mine, theirs], axis=1)
    came = [sent(both[k * tokens : (k + 1) * tokens], home_target(k)) for k in range(4)]
    width = mine.shape[1]
    own_first = core == 0
    sides = []
    for step in range(2):
        total = came[step] + came[2 + step]
        a, b = total[:, :width], total[:, width:]
        sides.append(
            jnp.concatenate([jnp.where(own_first, a, b), jnp.where(own_first, b, a)], axis=1)
        )
    even = lax.axis_index("zl") % 2 == 0
    projected = jnp.concatenate(
        [jnp.where(even, sides[0], sides[1]), jnp.where(even, sides[1], sides[0])], axis=1
    )
    state = residual + projected

    squares = jnp.sum(state * state, axis=1)[None]
    squares = sum([over_x(squares, mask) for mask in (1, 2, 3)], squares)
    squares = squares + over_zh(squares)
    normed = (state * lax.rsqrt(squares[0] / features + EPSILON)[:, None] * norm_gain).astype(
        jnp.bfloat16
    )

    first, second = summed_over_x(
        gathered(normed), [gate_weight, up_weight], [other_gate, other_up], jnp.bfloat16
    )
    half = 2 * tokens

    def activated(pair):
        gate, up = [
            s[:half] + over_zh(s[half:].astype(jnp.bfloat16)).astype(jnp.float32) for s in pair
        ]
        return (jax.nn.silu(gate) * up).astype(jnp.bfloat16)

    def spread(activation):
        return jnp.concatenate([activation, over_zh(activation)])

    one, two = spread(activated(first)), spread(activated(second))
    one3, two1 = over_x(one, 3), over_x(two, 1)
    one12 = over_x(jnp.concatenate([one, one3]), 1)
    two32 = over_x(jnp.concatenate([two, two1]), 3)
    block = one.shape[0]
    parts = {
        0: (one, two),
        3: (one3, two32[:block]),
        1: (one12[:block], two1),
        2: (one12[block:], two32[block:]),
    }
    line = 0.0
    for mask in MASKS:
        a, b = parts[mask]
        down = (dot(a, down_weight) + dot(b, other_down)).astype(jnp.bfloat16)
        line = line + sent(down, ring_target(mask)).astype(jnp.float32)
    line = line.astype(jnp.bfloat16)
    result = state
    for place in range(4):
        piece = line[place * tokens : (place + 1) * tokens]
        result = result + sent(piece, line_target(place)).astype(jnp.float32)
    return result


def solution(mesh):
    split = Mesh(mesh.devices.reshape(4, 4, 2, 4, 2), ("y", "zl", "zh", "x", "core"))
    all_rows = (*REQ, "core")
    in_specs = (
        P(REQ, None, KVH),
        P(REQ, None, KVH),
        P(REQ, None, KVH),
        P(REQ, KVH, "core", None),
        P(REQ, KVH, "core", None),
        P(),
        P(REQ, None),
        P(all_rows, KVH),
        P(KVH, all_rows),
        P(KVH),
        P(KVH, all_rows),
        P(KVH, all_rows),
        P(all_rows, KVH),
    )
    return jax.shard_map(
        local, mesh=split, in_specs=in_specs, out_specs=P(all_rows, KVH), check_vma=False
    )
```

```python
import jax
import jax.numpy as jnp
from jax import lax
from jax.experimental import pallas as pl
from jax.experimental.pallas import tpu as pltpu
from jax.sharding import Mesh
from jax.sharding import PartitionSpec as P

KB = 1024
REQ = ("y", "zl")
KVH = ("zh", "x")
GRID = ("y", "zl", "zh", "x")
SIZES = (4, 4, 2, 4)
MASKED = -1e30
EPSILON = 1e-05
MASKS = (0, 3, 1, 2)


def sent(array, target):
    pairs = []
    for source in range(128):
        x, zh, zl, y = source % 4, source // 4 % 2, source // 8 % 4, source // 32
        to = target(y, zl, zh, x)
        pairs.append((source, ((to[0] * 4 + to[1]) * 2 + to[2]) * 4 + to[3]))
    return lax.ppermute(array, GRID, pairs)


def over_x(array, mask):
    return lax.ppermute(array, "x", [(i, i ^ mask) for i in range(4)])


def over_zh(array):
    return lax.ppermute(array, "zh", [(0, 1), (1, 0)])


def over_core(array):
    return lax.ppermute(array, "core", [(0, 1), (1, 0)])


def line_target(place):
    part, step = divmod(place, 2)
    return lambda y, zl, zh, x: (y, zl ^ (2 * (part ^ zh) + step), zh, x)


def ring_target(mask):
    return lambda y, zl, zh, x: (y ^ x ^ mask, zl, zh, x)


def home_target(place):
    part, step = divmod(place, 2)
    return lambda y, zl, zh, x: (
        y ^ x,
        zl ^ (2 * (part ^ zh) + step),
        zl >> 1,
        y,
    )


def column_target(y, zl, zh, x):
    return 2 * (y & 1) + (zl >> 1), 2 * (y >> 1) + (zl & 1), zh, x


def gathered(rows):
    line = jnp.concatenate([sent(rows, line_target(place)) for place in range(4)])
    return {mask: sent(line, ring_target(mask)) for mask in MASKS}


def together(move, arrays, *how):
    joined = move(jnp.concatenate(arrays, axis=1), *how)
    cuts = [sum(a.shape[1] for a in arrays[: k + 1]) for k in range(len(arrays) - 1)]
    return jnp.split(joined, cuts, axis=1)


def dot(a, b):
    return jnp.dot(a, b, preferred_element_type=jnp.float32)


def summed_over_x(blocks, first, second, dtype):
    pair = lambda a, b: jnp.concatenate([blocks[a], blocks[b]])
    away1, away2 = pair(1, 2), pair(3, 2)
    stay1, stay2 = pair(0, 3), pair(0, 1)
    half = blocks[0].shape[0]
    got1 = together(over_x, [dot(away1, w).astype(dtype) for w in first], 1)
    got2 = together(over_x, [dot(away2, w).astype(dtype) for w in second], 3)
    sum1 = [dot(stay1, w) + g for w, g in zip(first, got1)]
    sum2 = [dot(stay2, w) + g for w, g in zip(second, got2)]
    got1 = together(over_x, [s[half:].astype(dtype) for s in sum1], 3)
    got2 = together(over_x, [s[half:].astype(dtype) for s in sum2], 1)
    return [
        [s[:half] + g for s, g in zip(sums, got)] for sums, got in ((sum1, got1), (sum2, got2))
    ]


def attend_kernel(
    info, queries, tree_keys, tree_values, parents, keys, values, own, other, rows, top, total, mix
):
    step, live, core = pl.program_id(0), info[0], info[1]
    nodes, width = queries.shape
    block, head = keys.shape
    heads = width // head
    scale = head**-0.5

    def scored(key_block):
        return scale * lax.dot_general(
            rows[...], key_block, (((1,), (1,)), ((), ())), preferred_element_type=jnp.float32
        )

    def mixed(weights, value_block):
        high = weights.astype(jnp.bfloat16)
        low = (weights - high.astype(jnp.float32)).astype(jnp.bfloat16)
        return dot(high, value_block) + dot(low, value_block)

    @pl.when(step == 0)
    def _():
        for j in range(heads):
            rows[j * nodes : (j + 1) * nodes, :] = queries[:, j * head : (j + 1) * head]

        @pl.when(core == 0)
        def _():
            places = lax.broadcasted_iota(jnp.int32, (nodes, nodes), 1)
            level = lax.broadcasted_iota(jnp.int32, (nodes, nodes), 0)
            reach = jnp.where((places == level) | (parents[...] == places), 1.0, 0.0)
            for _ in range((nodes - 1).bit_length()):
                reach = jnp.minimum(dot(reach.astype(jnp.bfloat16), reach.astype(jnp.bfloat16)), 1.0)
            reach = jnp.concatenate([reach] * heads)
            scores = jnp.where(reach > 0.5, scored(tree_keys[...]), MASKED)
            highest = jnp.max(scores, axis=1, keepdims=True)
            weights = jnp.exp(scores - highest)
            top[...] = jnp.broadcast_to(highest, top.shape)
            total[...] = jnp.broadcast_to(jnp.sum(weights, axis=1, keepdims=True), total.shape)
            mix[...] = mixed(weights, tree_values[...])

        @pl.when(core != 0)
        def _():
            top[...] = jnp.full(top.shape, MASKED, jnp.float32)
            total[...] = jnp.zeros(total.shape, jnp.float32)
            mix[...] = jnp.zeros(mix.shape, jnp.float32)

    @pl.when(step * block < live)
    def _():
        scores = scored(keys[...])
        positions = step * block + lax.broadcasted_iota(jnp.int32, scores.shape, 1)
        scores = jnp.where(positions < live, scores, MASKED)
        before = top[:, :1]
        highest = jnp.maximum(before, jnp.max(scores, axis=1, keepdims=True))
        weights = jnp.exp(scores - highest)
        factor = jnp.exp(before - highest)
        top[...] = jnp.broadcast_to(highest, top.shape)
        total[...] = total[...] * factor + jnp.sum(weights, axis=1, keepdims=True)
        mix[...] = mix[...] * factor + mixed(weights, values[...])

    @pl.when(step == pl.num_programs(0) - 1)
    def _():
        half = nodes // 2
        count = heads * half
        first = lax.broadcasted_iota(jnp.int32, (half, head), 1) < head // 2
        for side, out in ((core, own), (1 - core, other)):
            for j in range(heads):
                here = pl.ds(pl.multiple_of(j * nodes + side * half, half), half)
                out[j * half : (j + 1) * half, :] = mix[here, :]
                out[count + j * half : count + (j + 1) * half, :] = jnp.where(
                    first, top[here, :], total[here, :]
                )


def combine_kernel(own, came, out):
    half = out.shape[0]
    count, head = own.shape[0] // 2, own.shape[1]
    for j in range(count // half):
        here = slice(j * half, (j + 1) * half)
        numbers = slice(count + j * half, count + (j + 1) * half)
        top1, total1 = own[numbers, :1], own[numbers, head - 1 :]
        top2, total2 = came[numbers, :1], came[numbers, head - 1 :]
        highest = jnp.maximum(top1, top2)
        factor1, factor2 = jnp.exp(top1 - highest), jnp.exp(top2 - highest)
        total = total1 * factor1 + total2 * factor2
        value = (own[here, :] * factor1 + came[here, :] * factor2) / total
        out[:, j * head : (j + 1) * head] = value.astype(out.dtype)


def attended_parts(queries, tree_keys, tree_values, keys, values, length, parent_row, core):
    nodes, width = queries.shape
    half_len, head = keys.shape
    rows = width // head * nodes
    block = min(KB, half_len)
    live = jnp.clip(length - core * half_len, 0, half_len)
    info = jnp.stack([live, core]).astype(jnp.int32)
    whole = lambda shape: pl.BlockSpec(shape, lambda i, info: (0, 0))
    last = lambda i, info: (jnp.minimum(i, jnp.maximum(info[0] - 1, 0) // block), 0)
    side = jax.ShapeDtypeStruct((rows, head), jnp.float32)
    return pl.pallas_call(
        attend_kernel,
        out_shape=(side, side),
        grid_spec=pltpu.PrefetchScalarGridSpec(
            num_scalar_prefetch=1,
            grid=(half_len // block,),
            in_specs=[
                whole((nodes, width)),
                whole((nodes, head)),
                whole((nodes, head)),
                whole((nodes, 1)),
                pl.BlockSpec((block, head), last),
                pl.BlockSpec((block, head), last),
            ],
            out_specs=(whole((rows, head)), whole((rows, head))),
            scratch_shapes=[
                pltpu.VMEM((rows, head), jnp.bfloat16),
                pltpu.VMEM((rows, head), jnp.float32),
                pltpu.VMEM((rows, head), jnp.float32),
                pltpu.VMEM((rows, head), jnp.float32),
            ],
        ),
        compiler_params=pltpu.CompilerParams(vmem_limit_bytes=32 << 20),
        cost_estimate=pl.CostEstimate(
            flops=6 * rows * half_len * head,
            bytes_accessed=4 * half_len * head,
            transcendentals=rows * half_len,
        ),
        name="attend",
    )(info, queries, tree_keys, tree_values, parent_row[:, None], keys, values)


def attended(own, other, half):
    rows, head = own.shape
    return pl.pallas_call(
        combine_kernel,
        out_shape=jax.ShapeDtypeStruct((half, rows // 2 // half * head), jnp.bfloat16),
        name="combine",
    )(own, over_core(other))


def local(
    queries,
    tree_keys,
    tree_token_values,
    cache_keys,
    cached_value_rows,
    lengths,
    parents,
    residual,
    out_weight,
    norm_gain,
    gate_weight,
    up_weight,
    down_weight,
):
    core = lax.axis_index("core")
    features = norm_gain.shape[0] * 8
    out_weight = sent(out_weight, column_target)
    other_gate = over_core(gate_weight)
    other_up = over_core(up_weight)
    other_down = over_core(down_weight)
    length = lax.dynamic_index_in_dim(lengths, lax.axis_index(REQ), keepdims=False)
    parts = attended_parts(
        queries[0],
        tree_keys[0],
        tree_token_values[0],
        cache_keys[0, 0],
        cached_value_rows[0, 0],
        length,
        parents[0],
        core,
    )
    parts, out_weight, other_gate, other_up, other_down = lax.optimization_barrier(
        (parts, out_weight, other_gate, other_up, other_down)
    )
    attention = attended(*parts, queries.shape[1] // 2)
    other_out = over_core(out_weight)
    tokens = attention.shape[0]

    (mine,), (theirs,) = summed_over_x(
        gathered(attention), [out_weight], [other_out], jnp.float32
    )
    both = jnp.concatenate([mine, theirs], axis=1)
    came = [sent(both[k * tokens : (k + 1) * tokens], home_target(k)) for k in range(4)]
    width = mine.shape[1]
    own_first = core == 0
    sides = []
    for step in range(2):
        total = came[step] + came[2 + step]
        a, b = total[:, :width], total[:, width:]
        sides.append(
            jnp.concatenate([jnp.where(own_first, a, b), jnp.where(own_first, b, a)], axis=1)
        )
    even = lax.axis_index("zl") % 2 == 0
    projected = jnp.concatenate(
        [jnp.where(even, sides[0], sides[1]), jnp.where(even, sides[1], sides[0])], axis=1
    )
    state = residual + projected

    squares = jnp.sum(state * state, axis=1)[None]
    squares = sum([over_x(squares, mask) for mask in (1, 2, 3)], squares)
    squares = squares + over_zh(squares)
    normed = (state * lax.rsqrt(squares[0] / features + EPSILON)[:, None] * norm_gain).astype(
        jnp.bfloat16
    )

    first, second = summed_over_x(
        gathered(normed), [gate_weight, up_weight], [other_gate, other_up], jnp.bfloat16
    )
    half = 2 * tokens

    ours = first + second
    came = together(over_zh, [s[half:].astype(jnp.bfloat16) for s in ours])
    gate1, up1, gate2, up2 = [s[:half] + g for s, g in zip(ours, came)]
    active = [
        (jax.nn.silu(gate) * up).astype(jnp.bfloat16) for gate, up in ((gate1, up1), (gate2, up2))
    ]

    one, two = [
        jnp.concatenate([a, b]) for a, b in zip(active, together(over_zh, active))
    ]
    one3, two1 = over_x(one, 3), over_x(two, 1)
    one12 = over_x(jnp.concatenate([one, one3]), 1)
    two32 = over_x(jnp.concatenate([two, two1]), 3)
    block = one.shape[0]
    parts = {
        0: (one, two),
        3: (one3, two32[:block]),
        1: (one12[:block], two1),
        2: (one12[block:], two32[block:]),
    }
    line = 0.0
    for mask in MASKS:
        a, b = parts[mask]
        down = (dot(a, down_weight) + dot(b, other_down)).astype(jnp.bfloat16)
        line = line + sent(down, ring_target(mask)).astype(jnp.float32)
    line = line.astype(jnp.bfloat16)
    result = state
    for place in range(4):
        piece = line[place * tokens : (place + 1) * tokens]
        result = result + sent(piece, line_target(place)).astype(jnp.float32)
    return result


def solution(mesh):
    split = Mesh(mesh.devices.reshape(4, 4, 2, 4, 2), ("y", "zl", "zh", "x", "core"))
    all_rows = (*REQ, "core")
    in_specs = (
        P(REQ, None, KVH),
        P(REQ, None, KVH),
        P(REQ, None, KVH),
        P(REQ, KVH, "core", None),
        P(REQ, KVH, "core", None),
        P(),
        P(REQ, None),
        P(all_rows, KVH),
        P(KVH, all_rows),
        P(KVH),
        P(KVH, all_rows),
        P(KVH, all_rows),
        P(all_rows, KVH),
    )
    return jax.shard_map(
        local, mesh=split, in_specs=in_specs, out_specs=P(all_rows, KVH), check_vma=False
    )
```

```python
import jax
import jax.numpy as jnp
from jax import lax
from jax.experimental import pallas as pl
from jax.experimental.pallas import tpu as pltpu
from jax.sharding import Mesh
from jax.sharding import PartitionSpec as P

KB = 1024
REQ = ("y", "zl")
KVH = ("zh", "x")
GRID = ("y", "zl", "zh", "x")
SIZES = (4, 4, 2, 4)
MASKED = -1e30
EPSILON = 1e-05
MASKS = (0, 3, 1, 2)


def sent(array, target):
    pairs = []
    for source in range(128):
        x, zh, zl, y = source % 4, source // 4 % 2, source // 8 % 4, source // 32
        to = target(y, zl, zh, x)
        pairs.append((source, ((to[0] * 4 + to[1]) * 2 + to[2]) * 4 + to[3]))
    return lax.ppermute(array, GRID, pairs)


def over_x(array, mask):
    return lax.ppermute(array, "x", [(i, i ^ mask) for i in range(4)])


def over_zh(array):
    return lax.ppermute(array, "zh", [(0, 1), (1, 0)])


def over_core(array):
    return lax.ppermute(array, "core", [(0, 1), (1, 0)])


def line_target(place):
    part, step = divmod(place, 2)
    return lambda y, zl, zh, x: (y, zl ^ (2 * (part ^ zh) + step), zh, x)


def ring_target(mask):
    return lambda y, zl, zh, x: (y ^ x ^ mask, zl, zh, x)


def near_target(place):
    part, step = divmod(place, 2)
    return lambda y, zl, zh, x: (y, zl ^ (2 * (part ^ turn(x)) + step), zh, x)


def turn(x):
    return (x >> 1) ^ (x & 1)


def home_target(place):
    part, step = divmod(place, 2)
    return lambda y, zl, zh, x: (
        y,
        2 * (turn(x) ^ (zl >> 1)) + ((zl & 1) ^ step),
        zh ^ part,
        2 * (x >> 1) + (zl >> 1),
    )


def columns_over_y(weight):
    blocks = [weight] + [
        lax.ppermute(weight, "y", [(i, i ^ mask) for i in range(4)]) for mask in (2, 1, 3)
    ]
    return jnp.concatenate(blocks, axis=1)


def gathered(rows):
    line = jnp.concatenate([sent(rows, line_target(place)) for place in range(4)])
    return {mask: sent(line, ring_target(mask)) for mask in MASKS}


def together(move, arrays, *how):
    joined = move(jnp.concatenate(arrays, axis=1), *how)
    cuts = [sum(a.shape[1] for a in arrays[: k + 1]) for k in range(len(arrays) - 1)]
    return jnp.split(joined, cuts, axis=1)


def dot(a, b):
    return jnp.dot(a, b, preferred_element_type=jnp.float32)


def summed_over_x(blocks, first, second, dtype):
    pair = lambda a, b: jnp.concatenate([blocks[a], blocks[b]])
    away1, away2 = pair(1, 2), pair(3, 2)
    stay1, stay2 = pair(0, 3), pair(0, 1)
    half = blocks[0].shape[0]
    sides = [
        jnp.concatenate([dot(away, w).astype(dtype) for w in weights], axis=1)
        for away, weights in ((away1, first), (away2, second))
    ]
    sides = lax.optimization_barrier(sides)
    got1, got2 = [jnp.split(over_x(a, mask), 2, axis=1) for a, mask in zip(sides, (1, 3))]
    sum1 = [dot(stay1, w) + g for w, g in zip(first, got1)]
    sum2 = [dot(stay2, w) + g for w, g in zip(second, got2)]
    got1 = together(over_x, [s[half:].astype(dtype) for s in sum1], 3)
    got2 = together(over_x, [s[half:].astype(dtype) for s in sum2], 1)
    return [
        [s[:half] + g for s, g in zip(sums, got)] for sums, got in ((sum1, got1), (sum2, got2))
    ]


def attend_kernel(
    info, queries, tree_keys, tree_values, parents, keys, values, own, other, rows, top, total, mix
):
    step, live, core = pl.program_id(0), info[0], info[1]
    nodes, width = queries.shape
    block, head = keys.shape
    heads = width // head
    scale = head**-0.5

    def scored(key_block):
        return scale * lax.dot_general(
            rows[...], key_block, (((1,), (1,)), ((), ())), preferred_element_type=jnp.float32
        )

    def mixed(weights, value_block):
        high = weights.astype(jnp.bfloat16)
        low = (weights - high.astype(jnp.float32)).astype(jnp.bfloat16)
        return dot(high, value_block) + dot(low, value_block)

    @pl.when(step == 0)
    def _():
        for j in range(heads):
            rows[j * nodes : (j + 1) * nodes, :] = queries[:, j * head : (j + 1) * head]

        @pl.when(core == 0)
        def _():
            places = lax.broadcasted_iota(jnp.int32, (nodes, nodes), 1)
            level = lax.broadcasted_iota(jnp.int32, (nodes, nodes), 0)
            reach = jnp.where((places == level) | (parents[...] == places), 1.0, 0.0)
            for _ in range((nodes - 1).bit_length()):
                reach = jnp.minimum(dot(reach.astype(jnp.bfloat16), reach.astype(jnp.bfloat16)), 1.0)
            reach = jnp.concatenate([reach] * heads)
            scores = jnp.where(reach > 0.5, scored(tree_keys[...]), MASKED)
            highest = jnp.max(scores, axis=1, keepdims=True)
            weights = jnp.exp(scores - highest)
            top[...] = jnp.broadcast_to(highest, top.shape)
            total[...] = jnp.broadcast_to(jnp.sum(weights, axis=1, keepdims=True), total.shape)
            mix[...] = mixed(weights, tree_values[...])

        @pl.when(core != 0)
        def _():
            top[...] = jnp.full(top.shape, MASKED, jnp.float32)
            total[...] = jnp.zeros(total.shape, jnp.float32)
            mix[...] = jnp.zeros(mix.shape, jnp.float32)

    @pl.when(step * block < live)
    def _():
        scores = scored(keys[...])
        positions = step * block + lax.broadcasted_iota(jnp.int32, scores.shape, 1)
        scores = jnp.where(positions < live, scores, MASKED)
        before = top[:, :1]
        highest = jnp.maximum(before, jnp.max(scores, axis=1, keepdims=True))
        weights = jnp.exp(scores - highest)
        factor = jnp.exp(before - highest)
        top[...] = jnp.broadcast_to(highest, top.shape)
        total[...] = total[...] * factor + jnp.sum(weights, axis=1, keepdims=True)
        mix[...] = mix[...] * factor + mixed(weights, values[...])

    @pl.when(step == pl.num_programs(0) - 1)
    def _():
        half = nodes // 2
        count = heads * half
        first = lax.broadcasted_iota(jnp.int32, (half, head), 1) < head // 2
        for side, out in ((core, own), (1 - core, other)):
            for j in range(heads):
                here = pl.ds(pl.multiple_of(j * nodes + side * half, half), half)
                out[j * half : (j + 1) * half, :] = mix[here, :]
                out[count + j * half : count + (j + 1) * half, :] = jnp.where(
                    first, top[here, :], total[here, :]
                )


def combine_kernel(own, came, out):
    half = out.shape[0]
    count, head = own.shape[0] // 2, own.shape[1]
    for j in range(count // half):
        here = slice(j * half, (j + 1) * half)
        numbers = slice(count + j * half, count + (j + 1) * half)
        top1, total1 = own[numbers, :1], own[numbers, head - 1 :]
        top2, total2 = came[numbers, :1], came[numbers, head - 1 :]
        highest = jnp.maximum(top1, top2)
        factor1, factor2 = jnp.exp(top1 - highest), jnp.exp(top2 - highest)
        total = total1 * factor1 + total2 * factor2
        value = (own[here, :] * factor1 + came[here, :] * factor2) / total
        out[:, j * head : (j + 1) * head] = value.astype(out.dtype)


def attended_parts(queries, tree_keys, tree_values, keys, values, length, parent_row, core):
    nodes, width = queries.shape
    half_len, head = keys.shape
    rows = width // head * nodes
    block = min(KB, half_len)
    live = jnp.clip(length - core * half_len, 0, half_len)
    info = jnp.stack([live, core]).astype(jnp.int32)
    whole = lambda shape: pl.BlockSpec(shape, lambda i, info: (0, 0))
    last = lambda i, info: (jnp.minimum(i, jnp.maximum(info[0] - 1, 0) // block), 0)
    side = jax.ShapeDtypeStruct((rows, head), jnp.float32)
    return pl.pallas_call(
        attend_kernel,
        out_shape=(side, side),
        grid_spec=pltpu.PrefetchScalarGridSpec(
            num_scalar_prefetch=1,
            grid=(half_len // block,),
            in_specs=[
                whole((nodes, width)),
                whole((nodes, head)),
                whole((nodes, head)),
                whole((nodes, 1)),
                pl.BlockSpec((block, head), last),
                pl.BlockSpec((block, head), last),
            ],
            out_specs=(whole((rows, head)), whole((rows, head))),
            scratch_shapes=[
                pltpu.VMEM((rows, head), jnp.bfloat16),
                pltpu.VMEM((rows, head), jnp.float32),
                pltpu.VMEM((rows, head), jnp.float32),
                pltpu.VMEM((rows, head), jnp.float32),
            ],
        ),
        compiler_params=pltpu.CompilerParams(vmem_limit_bytes=56 << 20),
        cost_estimate=pl.CostEstimate(
            flops=6 * rows * half_len * head,
            bytes_accessed=4 * half_len * head,
            transcendentals=rows * half_len,
        ),
        name="attend",
    )(info, queries, tree_keys, tree_values, parent_row[:, None], keys, values)


def attended(own, other, half):
    rows, head = own.shape
    return pl.pallas_call(
        combine_kernel,
        out_shape=jax.ShapeDtypeStruct((half, rows // 2 // half * head), jnp.bfloat16),
        name="combine",
    )(own, over_core(other))


def local(
    queries,
    tree_keys,
    tree_token_values,
    cache_keys,
    cached_value_rows,
    lengths,
    parents,
    residual,
    out_weight,
    norm_gain,
    gate_weight,
    up_weight,
    down_weight,
):
    core = lax.axis_index("core")
    features = norm_gain.shape[0] * 8
    out_weight = columns_over_y(out_weight)
    other_gate = over_core(gate_weight)
    other_up = over_core(up_weight)
    length = lax.dynamic_index_in_dim(lengths, lax.axis_index(REQ), keepdims=False)
    parts = attended_parts(
        queries[0],
        tree_keys[0],
        tree_token_values[0],
        cache_keys[0, 0],
        cached_value_rows[0, 0],
        length,
        parents[0],
        core,
    )
    parts, out_weight, other_gate, other_up = lax.optimization_barrier(
        (parts, out_weight, other_gate, other_up)
    )
    attention = attended(*parts, queries.shape[1] // 2)
    other_out = over_core(out_weight)
    tokens = attention.shape[0]

    rows = jnp.concatenate([sent(attention, near_target(place)) for place in range(4)])
    rows, out_weight, other_out = lax.optimization_barrier((rows, out_weight, other_out))
    y, zh, x = [lax.axis_index(name) for name in ("y", "zh", "x")]
    odd = ((y & 1) ^ (x >> 1)) == 1

    def classes(products):
        half = products.shape[1] // 2
        a, b = products[:, :half], products[:, half:]
        return jnp.where(odd, b, a), jnp.where(odd, a, b)

    half = 2 * tokens
    mine_stay, mine_away = classes(dot(rows, out_weight))
    theirs = dot(rows, other_out)
    mine_away, theirs_away = lax.optimization_barrier((mine_away, theirs[half:]))
    mine_came, theirs_came = over_x(mine_away, 3), over_x(theirs_away, 1)
    mine = mine_stay + mine_came
    mine_came = over_x(mine[half:], 1)
    theirs_stay, theirs_away = classes(theirs[:half] + theirs_came)
    theirs_came = over_x(theirs_away, 3)
    mine = mine[:half] + mine_came
    theirs = theirs_stay + theirs_came
    width = mine.shape[1] // 2
    swap = (zh ^ (y >> 1)) == 1

    def item(part, step):
        near, far = [
            jnp.concatenate([a[step * tokens : (step + 1) * tokens, k * width : (k + 1) * width] for a in (mine, theirs)], axis=1)
            for k in (part, 1 - part)
        ]
        return jnp.where(swap, far, near)

    came = [sent(item(*divmod(place, 2)), home_target(place)) for place in range(4)]
    own_first = core == 0
    sides = []
    for step in range(2):
        total = came[step] + came[2 + step]
        a, b = total[:, :width], total[:, width:]
        sides.append(
            jnp.concatenate([jnp.where(own_first, a, b), jnp.where(own_first, b, a)], axis=1)
        )
    even = lax.axis_index("zl") % 2 == 0
    projected = jnp.concatenate(
        [jnp.where(even, sides[0], sides[1]), jnp.where(even, sides[1], sides[0])], axis=1
    )
    state = residual + projected

    squares = jnp.broadcast_to(jnp.sum(state * state, axis=1), (8, 1, tokens))
    squares = lax.all_to_all(squares, KVH, 0, 0, tiled=True).sum(axis=(0, 1))
    normed = (state * lax.rsqrt(squares / features + EPSILON)[:, None] * norm_gain).astype(
        jnp.bfloat16
    )

    other_down = over_core(down_weight)

    first, second = summed_over_x(
        gathered(normed), [gate_weight, up_weight], [other_gate, other_up], jnp.bfloat16
    )
    half = 2 * tokens

    ours = first + second
    came = together(over_zh, [s[half:].astype(jnp.bfloat16) for s in ours])
    gate1, up1, gate2, up2 = [s[:half] + g for s, g in zip(ours, came)]
    active = [
        (jax.nn.silu(gate) * up).astype(jnp.bfloat16) for gate, up in ((gate1, up1), (gate2, up2))
    ]

    one, two = [
        jnp.concatenate([a, b]) for a, b in zip(active, together(over_zh, active))
    ]
    one3, two1 = over_x(one, 3), over_x(two, 1)
    one12 = over_x(jnp.concatenate([one, one3]), 1)
    two32 = over_x(jnp.concatenate([two, two1]), 3)
    block = one.shape[0]
    parts = {
        0: (one, two),
        3: (one3, two32[:block]),
        1: (one12[:block], two1),
        2: (one12[block:], two32[block:]),
    }
    line = 0.0
    for mask in MASKS:
        a, b = parts[mask]
        down = (dot(a, down_weight) + dot(b, other_down)).astype(jnp.bfloat16)
        line = line + sent(down, ring_target(mask)).astype(jnp.float32)
    line = line.astype(jnp.bfloat16)
    result = state
    for place in range(4):
        piece = line[place * tokens : (place + 1) * tokens]
        result = result + sent(piece, line_target(place)).astype(jnp.float32)
    return result


def solution(mesh):
    split = Mesh(mesh.devices.reshape(4, 4, 2, 4, 2), ("y", "zl", "zh", "x", "core"))
    all_rows = (*REQ, "core")
    in_specs = (
        P(REQ, None, KVH),
        P(REQ, None, KVH),
        P(REQ, None, KVH),
        P(REQ, KVH, "core", None),
        P(REQ, KVH, "core", None),
        P(),
        P(REQ, None),
        P(all_rows, KVH),
        P(KVH, all_rows),
        P(KVH),
        P(KVH, all_rows),
        P(KVH, all_rows),
        P(all_rows, KVH),
    )
    return jax.shard_map(
        local, mesh=split, in_specs=in_specs, out_specs=P(all_rows, KVH), check_vma=False
    )
```

```python
import math

import jax
import jax.numpy as jnp
from jax import lax
from jax.experimental import pallas as pl
from jax.experimental.pallas import tpu as pltpu
from jax.sharding import Mesh
from jax.sharding import PartitionSpec as P

KB = 1024
REQ = ("y", "zl")
KVH = ("zh", "x")
GRID = ("y", "zl", "zh", "x")
SIZES = (4, 4, 2, 4)
MASKED = -1e30
EPSILON = 1e-05
MASKS = (0, 3, 1, 2)


def sent(array, target):
    pairs = []
    for source in range(128):
        x, zh, zl, y = source % 4, source // 4 % 2, source // 8 % 4, source // 32
        to = target(y, zl, zh, x)
        pairs.append((source, ((to[0] * 4 + to[1]) * 2 + to[2]) * 4 + to[3]))
    return lax.ppermute(array, GRID, pairs)


def over_x(array, mask):
    return lax.ppermute(array, "x", [(i, i ^ mask) for i in range(4)])


def over_zh(array):
    return lax.ppermute(array, "zh", [(0, 1), (1, 0)])


def over_core(array):
    return lax.ppermute(array, "core", [(0, 1), (1, 0)])


def line_target(place):
    part, step = divmod(place, 2)
    return lambda y, zl, zh, x: (y, zl ^ (2 * (part ^ zh) + step), zh, x)


def ring_target(mask):
    return lambda y, zl, zh, x: (y ^ x ^ mask, zl, zh, x)


def near_target(place):
    part, step = divmod(place, 2)
    return lambda y, zl, zh, x: (y, zl ^ (2 * (part ^ turn(x)) + step), zh, x)


def turn(x):
    return (x >> 1) ^ (x & 1)


def home_target(place):
    part, step = divmod(place, 2)
    return lambda y, zl, zh, x: (
        y,
        2 * (turn(x) ^ (zl >> 1)) + ((zl & 1) ^ step),
        zh ^ part,
        2 * (x >> 1) + (zl >> 1),
    )


def over_y(array, mask):
    return lax.ppermute(array, "y", [(i, i ^ mask) for i in range(4)])


def gathered(rows):
    line = jnp.concatenate([sent(rows, line_target(place)) for place in range(4)])
    return {mask: sent(line, ring_target(mask)) for mask in MASKS}


def together(move, arrays, *how):
    joined = move(jnp.concatenate(arrays, axis=1), *how)
    cuts = [sum(a.shape[1] for a in arrays[: k + 1]) for k in range(len(arrays) - 1)]
    return jnp.split(joined, cuts, axis=1)


def dot(a, b):
    return jnp.dot(a, b, preferred_element_type=jnp.float32)


def summed_over_x(blocks, first, second, dtype):
    pair = lambda a, b: jnp.concatenate([blocks[a], blocks[b]])
    away1, away2 = pair(1, 2), pair(3, 2)
    stay1, stay2 = pair(0, 3), pair(0, 1)
    half = blocks[0].shape[0]
    sides = [
        jnp.concatenate([dot(away, w).astype(dtype) for w in weights], axis=1)
        for away, weights in ((away1, first), (away2, second))
    ]
    sides = lax.optimization_barrier(sides)
    got1, got2 = [jnp.split(over_x(a, mask), 2, axis=1) for a, mask in zip(sides, (1, 3))]
    sum1 = [dot(stay1, w) + g for w, g in zip(first, got1)]
    sum2 = [dot(stay2, w) + g for w, g in zip(second, got2)]
    got1 = together(over_x, [s[half:].astype(dtype) for s in sum1], 3)
    got2 = together(over_x, [s[half:].astype(dtype) for s in sum2], 1)
    return [
        [s[:half] + g for s, g in zip(sums, got)] for sums, got in ((sum1, got1), (sum2, got2))
    ]


def live_positions(place, lengths, half_len):
    return jnp.clip(lengths[place[0]] - place[1] * half_len, 0, half_len)


def attend_kernel(
    place, lengths, queries, tree_keys, tree_values, parents, keys, values, own, other, rows, top, total, mix
):
    step, core = pl.program_id(0), place[1]
    nodes, width = queries.shape
    block, head = keys.shape
    live = live_positions(place, lengths, block * pl.num_programs(0))
    heads = width // head
    scale = head**-0.5 * math.log2(math.e)

    def scored(key_block):
        return scale * lax.dot_general(
            rows[...], key_block, (((1,), (1,)), ((), ())), preferred_element_type=jnp.float32
        )

    def mixed(weights, value_block):
        high = weights.astype(jnp.bfloat16)
        low = (weights - high.astype(jnp.float32)).astype(jnp.bfloat16)
        return dot(high, value_block) + dot(low, value_block)

    @pl.when(step == 0)
    def _():
        for j in range(heads):
            rows[j * nodes : (j + 1) * nodes, :] = queries[:, j * head : (j + 1) * head]

        @pl.when(core == 0)
        def _():
            places = lax.broadcasted_iota(jnp.int32, (nodes, nodes), 1)
            level = lax.broadcasted_iota(jnp.int32, (nodes, nodes), 0)
            reach = jnp.where((places == level) | (parents[...] == places), 1.0, 0.0)
            for _ in range((nodes - 1).bit_length()):
                reach = jnp.minimum(dot(reach.astype(jnp.bfloat16), reach.astype(jnp.bfloat16)), 1.0)
            reach = jnp.concatenate([reach] * heads)
            scores = jnp.where(reach > 0.5, scored(tree_keys[...]), MASKED)
            highest = jnp.max(scores, axis=1, keepdims=True)
            weights = jnp.exp2(scores - highest)
            top[...] = jnp.broadcast_to(highest, top.shape)
            total[...] = jnp.broadcast_to(jnp.sum(weights, axis=1, keepdims=True), total.shape)
            mix[...] = mixed(weights, tree_values[...])

        @pl.when(core != 0)
        def _():
            top[...] = jnp.full(top.shape, MASKED, jnp.float32)
            total[...] = jnp.zeros(total.shape, jnp.float32)
            mix[...] = jnp.zeros(mix.shape, jnp.float32)

    def absorb(scores):
        before = top[:, :1]
        highest = jnp.maximum(before, jnp.max(scores, axis=1, keepdims=True))
        weights = jnp.exp2(scores - highest)
        factor = jnp.exp2(before - highest)
        top[...] = jnp.broadcast_to(highest, top.shape)
        total[...] = total[...] * factor + jnp.sum(weights, axis=1, keepdims=True)
        mix[...] = mix[...] * factor + mixed(weights, values[...])

    @pl.when((step + 1) * block <= live)
    def _():
        absorb(scored(keys[...]))

    @pl.when((step * block < live) & (live < (step + 1) * block))
    def _():
        positions = step * block + lax.broadcasted_iota(jnp.int32, (rows.shape[0], block), 1)
        absorb(jnp.where(positions < live, scored(keys[...]), MASKED))

    @pl.when(step == pl.num_programs(0) - 1)
    def _():
        half = nodes // 2
        count = heads * half
        first = lax.broadcasted_iota(jnp.int32, (half, head), 1) < head // 2
        for side, out in ((core, own), (1 - core, other)):
            for j in range(heads):
                here = pl.ds(pl.multiple_of(j * nodes + side * half, half), half)
                out[j * half : (j + 1) * half, :] = mix[here, :]
                out[count + j * half : count + (j + 1) * half, :] = jnp.where(
                    first, top[here, :], total[here, :]
                )


def combine_kernel(own, came, out):
    half = out.shape[0]
    count, head = own.shape[0] // 2, own.shape[1]
    for j in range(count // half):
        here = slice(j * half, (j + 1) * half)
        numbers = slice(count + j * half, count + (j + 1) * half)
        top1, total1 = own[numbers, :1], own[numbers, head - 1 :]
        top2, total2 = came[numbers, :1], came[numbers, head - 1 :]
        highest = jnp.maximum(top1, top2)
        factor1, factor2 = jnp.exp2(top1 - highest), jnp.exp2(top2 - highest)
        total = total1 * factor1 + total2 * factor2
        value = (own[here, :] * factor1 + came[here, :] * factor2) / total
        out[:, j * head : (j + 1) * head] = value.astype(out.dtype)


def attended_parts(queries, tree_keys, tree_values, keys, values, lengths, parent_row):
    nodes, width = queries.shape
    half_len, head = keys.shape
    rows = width // head * nodes
    block = min(KB, half_len)
    place = jnp.stack([lax.axis_index(REQ), lax.axis_index("core")]).astype(jnp.int32)
    whole = lambda shape: pl.BlockSpec(shape, lambda i, place, lengths: (0, 0))

    def last(i, place, lengths):
        live = live_positions(place, lengths, half_len)
        return jnp.minimum(i, jnp.maximum(live - 1, 0) // block), 0

    side = jax.ShapeDtypeStruct((rows, head), jnp.float32)
    return pl.pallas_call(
        attend_kernel,
        out_shape=(side, side),
        grid_spec=pltpu.PrefetchScalarGridSpec(
            num_scalar_prefetch=2,
            grid=(half_len // block,),
            in_specs=[
                whole((nodes, width)),
                whole((nodes, head)),
                whole((nodes, head)),
                whole((nodes, 1)),
                pl.BlockSpec((block, head), last),
                pl.BlockSpec((block, head), last),
            ],
            out_specs=(whole((rows, head)), whole((rows, head))),
            scratch_shapes=[
                pltpu.VMEM((rows, head), jnp.bfloat16),
                pltpu.VMEM((rows, head), jnp.float32),
                pltpu.VMEM((rows, head), jnp.float32),
                pltpu.VMEM((rows, head), jnp.float32),
            ],
        ),
        compiler_params=pltpu.CompilerParams(vmem_limit_bytes=56 << 20),
        cost_estimate=pl.CostEstimate(
            flops=6 * rows * half_len * head,
            bytes_accessed=4 * half_len * head,
            transcendentals=rows * half_len,
        ),
        name="attend",
    )(place, lengths, queries, tree_keys, tree_values, parent_row[:, None], keys, values)


def attended(own, came, half):
    rows, head = own.shape
    return pl.pallas_call(
        combine_kernel,
        out_shape=jax.ShapeDtypeStruct((half, rows // 2 // half * head), jnp.bfloat16),
        compiler_params=pltpu.CompilerParams(vmem_limit_bytes=8 << 20),
        name="combine",
    )(own, came)


def local(
    queries,
    tree_keys,
    tree_token_values,
    cache_keys,
    cached_value_rows,
    lengths,
    parents,
    residual,
    out_weight,
    norm_gain,
    gate_weight,
    up_weight,
    down_weight,
):
    core = lax.axis_index("core")
    features = norm_gain.shape[0] * 8
    columns = [over_y(out_weight, mask) for mask in (1, 3, 2)]
    other_gate = over_core(gate_weight)
    other_up = over_core(up_weight)
    length = lax.dynamic_index_in_dim(lengths, lax.axis_index(REQ), keepdims=False)
    parts = attended_parts(
        queries[0],
        tree_keys[0],
        tree_token_values[0],
        cache_keys[0, 0],
        cached_value_rows[0, 0],
        lengths,
        parents[0],
    )
    own, came, near1, near3, other0 = lax.optimization_barrier(
        (parts[0], over_core(parts[1]), *columns[:2], over_core(out_weight))
    )
    attention = attended(own, came, queries.shape[1] // 2)
    attention, other1, other3 = lax.optimization_barrier(
        (attention, over_core(near1), over_core(near3))
    )
    tokens = attention.shape[0]

    rows = [sent(attention, near_target(place)) for place in range(4)]
    *rows, farthest = lax.optimization_barrier((*rows, columns[2]))
    out_weight = jnp.concatenate([out_weight, farthest, near1, near3], axis=1)
    other_out = jnp.concatenate([other0, over_core(farthest), other1, other3], axis=1)
    rows, *weights = lax.optimization_barrier(
        (jnp.concatenate(rows), gate_weight, up_weight, down_weight)
    )
    other_gate, other_up, other_down = [over_core(weight) for weight in weights]
    core, y, zh, x = [lax.axis_index(name) for name in ("core", "y", "zh", "x")]
    odd = ((y & 1) ^ (x >> 1)) == 1

    def classes(products):
        half = products.shape[1] // 2
        a, b = products[:, :half], products[:, half:]
        return jnp.where(odd, b, a), jnp.where(odd, a, b)

    half = 2 * tokens
    mine_stay, mine_away = classes(dot(rows, out_weight))
    theirs = dot(rows, other_out)
    mine_away, theirs_away = lax.optimization_barrier((mine_away, theirs[half:]))
    mine_came, theirs_came = over_x(mine_away, 3), over_x(theirs_away, 1)
    mine = mine_stay + mine_came
    mine_came = over_x(mine[half:], 1)
    theirs_stay, theirs_away = classes(theirs[:half] + theirs_came)
    theirs_came = over_x(theirs_away, 3)
    mine = mine[:half] + mine_came
    theirs = theirs_stay + theirs_came
    mine, theirs, other_gate, other_up, other_down = lax.optimization_barrier(
        (mine, theirs, other_gate, other_up, other_down)
    )
    width = mine.shape[1] // 2
    swap = (zh ^ (y >> 1)) == 1

    def item(part, step):
        near, far = [
            jnp.concatenate([a[step * tokens : (step + 1) * tokens, k * width : (k + 1) * width] for a in (mine, theirs)], axis=1)
            for k in (part, 1 - part)
        ]
        return jnp.where(swap, far, near)

    came = [sent(item(*divmod(place, 2)), home_target(place)) for place in range(4)]
    own_first = core == 0
    sides = []
    for step in range(2):
        total = came[step] + came[2 + step]
        a, b = total[:, :width], total[:, width:]
        sides.append(
            jnp.concatenate([jnp.where(own_first, a, b), jnp.where(own_first, b, a)], axis=1)
        )
    even = lax.axis_index("zl") % 2 == 0
    projected = jnp.concatenate(
        [jnp.where(even, sides[0], sides[1]), jnp.where(even, sides[1], sides[0])], axis=1
    )
    state = residual + projected

    squares = jnp.broadcast_to(jnp.sum(state * state, axis=1), (8, 1, tokens))
    squares = lax.all_to_all(squares, KVH, 0, 0, tiled=True).sum(axis=(0, 1))
    normed = (state * lax.rsqrt(squares / features + EPSILON)[:, None] * norm_gain).astype(
        jnp.bfloat16
    )

    first, second = summed_over_x(
        gathered(normed), [gate_weight, up_weight], [other_gate, other_up], jnp.bfloat16
    )
    half = 2 * tokens

    ours = first + second
    came = together(over_zh, [s[half:].astype(jnp.bfloat16) for s in ours])
    gate1, up1, gate2, up2 = [s[:half] + g for s, g in zip(ours, came)]
    active = [
        (jax.nn.silu(gate) * up).astype(jnp.bfloat16) for gate, up in ((gate1, up1), (gate2, up2))
    ]

    one, two = [
        jnp.concatenate([a, b]) for a, b in zip(active, together(over_zh, active))
    ]
    one3, two1 = over_x(one, 3), over_x(two, 1)
    one12 = over_x(jnp.concatenate([one, one3]), 1)
    two32 = over_x(jnp.concatenate([two, two1]), 3)
    block = one.shape[0]
    parts = {
        0: (one, two),
        3: (one3, two32[:block]),
        1: (one12[:block], two1),
        2: (one12[block:], two32[block:]),
    }
    line = 0.0
    for mask in MASKS:
        a, b = parts[mask]
        down = (dot(a, down_weight) + dot(b, other_down)).astype(jnp.bfloat16)
        line = line + sent(down, ring_target(mask)).astype(jnp.float32)
    line = line.astype(jnp.bfloat16)
    result = state
    for place in range(4):
        piece = line[place * tokens : (place + 1) * tokens]
        result = result + sent(piece, line_target(place)).astype(jnp.float32)
    return result


def solution(mesh):
    split = Mesh(mesh.devices.reshape(4, 4, 2, 4, 2), ("y", "zl", "zh", "x", "core"))
    all_rows = (*REQ, "core")
    in_specs = (
        P(REQ, None, KVH),
        P(REQ, None, KVH),
        P(REQ, None, KVH),
        P(REQ, KVH, "core", None),
        P(REQ, KVH, "core", None),
        P(),
        P(REQ, None),
        P(all_rows, KVH),
        P(KVH, all_rows),
        P(KVH),
        P(KVH, all_rows),
        P(KVH, all_rows),
        P(all_rows, KVH),
    )
    return jax.shard_map(
        local, mesh=split, in_specs=in_specs, out_specs=P(all_rows, KVH), check_vma=False
    )
```

```python
import math

import jax
import jax.numpy as jnp
from jax import lax
from jax.experimental import pallas as pl
from jax.experimental.pallas import tpu as pltpu
from jax.sharding import Mesh
from jax.sharding import PartitionSpec as P

KB = 1024
REQ = ("y", "zl")
KVH = ("zh", "x")
GRID = ("y", "zl", "zh", "x")
SIZES = (4, 4, 2, 4)
MASKED = -1e30
EPSILON = 1e-05


def sent(array, target):
    pairs = []
    for source in range(128):
        x, zh, zl, y = source % 4, source // 4 % 2, source // 8 % 4, source // 32
        to = target(y, zl, zh, x)
        pairs.append((source, ((to[0] * 4 + to[1]) * 2 + to[2]) * 4 + to[3]))
    return lax.ppermute(array, GRID, pairs)


def over_x(array, mask):
    return lax.ppermute(array, "x", [(i, i ^ mask) for i in range(4)])


def over_zh(array):
    return lax.ppermute(array, "zh", [(0, 1), (1, 0)])


def over_core(array):
    return lax.ppermute(array, "core", [(0, 1), (1, 0)])


def turn(x):
    return (x >> 1) ^ (x & 1)


def home_target(place):
    part, step = divmod(place, 2)
    return lambda y, zl, zh, x: (
        y,
        2 * (turn(x) ^ (zl >> 1)) + ((zl & 1) ^ step),
        zh ^ part,
        2 * (x >> 1) + (zl >> 1),
    )


def over_y(array, mask):
    return lax.ppermute(array, "y", [(i, i ^ mask) for i in range(4)])


def over_zl(array, mask):
    return lax.ppermute(array, "zl", [(i, i ^ mask) for i in range(4)])


def halves_in_order(array, turned):
    half = array.shape[0] // 2
    return jnp.where(turned, jnp.concatenate([array[half:], array[:half]]), array)


def from_all_zl(rows, turned):
    return halves_in_order(
        jnp.concatenate([rows] + [over_zl(rows, mask) for mask in (1, 2, 3)]), turned
    )


def from_all_y(line, places):
    blocks = jnp.stack([line] + [over_y(line, mask) for mask in (1, 2, 3)])
    return [lax.dynamic_index_in_dim(blocks, place, keepdims=False) for place in places]


def together(move, arrays, *how):
    joined = move(jnp.concatenate(arrays, axis=1), *how)
    cuts = [sum(a.shape[1] for a in arrays[: k + 1]) for k in range(len(arrays) - 1)]
    return jnp.split(joined, cuts, axis=1)


def dot(a, b):
    return jnp.dot(a, b, preferred_element_type=jnp.float32)


def summed_over_x(blocks, first, second, dtype):
    pair = lambda a, b: jnp.concatenate([blocks[a], blocks[b]])
    away1, away2 = pair(1, 2), pair(3, 2)
    stay1, stay2 = pair(0, 3), pair(0, 1)
    half = blocks[0].shape[0]
    sides = [
        jnp.concatenate([dot(away, w).astype(dtype) for w in weights], axis=1)
        for away, weights in ((away1, first), (away2, second))
    ]
    sides = lax.optimization_barrier(sides)
    got1, got2 = [jnp.split(over_x(a, mask), 2, axis=1) for a, mask in zip(sides, (1, 3))]
    sum1 = [dot(stay1, w) + g for w, g in zip(first, got1)]
    sum2 = [dot(stay2, w) + g for w, g in zip(second, got2)]
    got1 = together(over_x, [s[half:].astype(dtype) for s in sum1], 3)
    got2 = together(over_x, [s[half:].astype(dtype) for s in sum2], 1)
    return [
        [s[:half] + g for s, g in zip(sums, got)] for sums, got in ((sum1, got1), (sum2, got2))
    ]


def live_positions(place, lengths, half_len):
    return jnp.clip(lengths[place[0]] - place[1] * half_len, 0, half_len)


def attend_kernel(
    place, lengths, queries, tree_keys, tree_values, parents, keys, values, own, other, rows, top, total, mix
):
    step, core = pl.program_id(0), place[1]
    nodes, width = queries.shape
    block, head = keys.shape
    live = live_positions(place, lengths, block * pl.num_programs(0))
    heads = width // head
    scale = head**-0.5 * math.log2(math.e)

    def scored(key_block):
        return scale * lax.dot_general(
            rows[...], key_block, (((1,), (1,)), ((), ())), preferred_element_type=jnp.float32
        )

    def mixed(weights, value_block):
        high = weights.astype(jnp.bfloat16)
        low = (weights - high.astype(jnp.float32)).astype(jnp.bfloat16)
        return dot(high, value_block) + dot(low, value_block)

    @pl.when(step == 0)
    def _():
        for j in range(heads):
            rows[j * nodes : (j + 1) * nodes, :] = queries[:, j * head : (j + 1) * head]

        @pl.when(core == 0)
        def _():
            places = lax.broadcasted_iota(jnp.int32, (nodes, nodes), 1)
            level = lax.broadcasted_iota(jnp.int32, (nodes, nodes), 0)
            reach = jnp.where((places == level) | (parents[...] == places), 1.0, 0.0)
            for _ in range((nodes - 1).bit_length()):
                reach = jnp.minimum(dot(reach.astype(jnp.bfloat16), reach.astype(jnp.bfloat16)), 1.0)
            reach = jnp.concatenate([reach] * heads)
            scores = jnp.where(reach > 0.5, scored(tree_keys[...]), MASKED)
            highest = jnp.max(scores, axis=1, keepdims=True)
            weights = jnp.exp2(scores - highest)
            top[...] = jnp.broadcast_to(highest, top.shape)
            total[...] = jnp.broadcast_to(jnp.sum(weights, axis=1, keepdims=True), total.shape)
            mix[...] = mixed(weights, tree_values[...])

        @pl.when(core != 0)
        def _():
            top[...] = jnp.full(top.shape, MASKED, jnp.float32)
            total[...] = jnp.zeros(total.shape, jnp.float32)
            mix[...] = jnp.zeros(mix.shape, jnp.float32)

    def absorb(scores):
        before = top[:, :1]
        highest = jnp.maximum(before, jnp.max(scores, axis=1, keepdims=True))
        weights = jnp.exp2(scores - highest)
        factor = jnp.exp2(before - highest)
        top[...] = jnp.broadcast_to(highest, top.shape)
        total[...] = total[...] * factor + jnp.sum(weights, axis=1, keepdims=True)
        mix[...] = mix[...] * factor + mixed(weights, values[...])

    @pl.when((step + 1) * block <= live)
    def _():
        absorb(scored(keys[...]))

    @pl.when((step * block < live) & (live < (step + 1) * block))
    def _():
        positions = step * block + lax.broadcasted_iota(jnp.int32, (rows.shape[0], block), 1)
        absorb(jnp.where(positions < live, scored(keys[...]), MASKED))

    @pl.when(step == pl.num_programs(0) - 1)
    def _():
        half = nodes // 2
        count = heads * half
        first = lax.broadcasted_iota(jnp.int32, (half, head), 1) < head // 2
        for side, out in ((core, own), (1 - core, other)):
            for j in range(heads):
                here = pl.ds(pl.multiple_of(j * nodes + side * half, half), half)
                out[j * half : (j + 1) * half, :] = mix[here, :]
                out[count + j * half : count + (j + 1) * half, :] = jnp.where(
                    first, top[here, :], total[here, :]
                )


def combine_kernel(own, came, out):
    half = out.shape[0]
    count, head = own.shape[0] // 2, own.shape[1]
    for j in range(count // half):
        here = slice(j * half, (j + 1) * half)
        numbers = slice(count + j * half, count + (j + 1) * half)
        top1, total1 = own[numbers, :1], own[numbers, head - 1 :]
        top2, total2 = came[numbers, :1], came[numbers, head - 1 :]
        highest = jnp.maximum(top1, top2)
        factor1, factor2 = jnp.exp2(top1 - highest), jnp.exp2(top2 - highest)
        total = total1 * factor1 + total2 * factor2
        value = (own[here, :] * factor1 + came[here, :] * factor2) / total
        out[:, j * head : (j + 1) * head] = value.astype(out.dtype)


def attended_parts(queries, tree_keys, tree_values, keys, values, lengths, parent_row):
    nodes, width = queries.shape
    half_len, head = keys.shape
    rows = width // head * nodes
    block = min(KB, half_len)
    place = jnp.stack([lax.axis_index(REQ), lax.axis_index("core")]).astype(jnp.int32)
    whole = lambda shape: pl.BlockSpec(shape, lambda i, place, lengths: (0, 0))

    def last(i, place, lengths):
        live = live_positions(place, lengths, half_len)
        return jnp.minimum(i, jnp.maximum(live - 1, 0) // block), 0

    side = jax.ShapeDtypeStruct((rows, head), jnp.float32)
    return pl.pallas_call(
        attend_kernel,
        out_shape=(side, side),
        grid_spec=pltpu.PrefetchScalarGridSpec(
            num_scalar_prefetch=2,
            grid=(half_len // block,),
            in_specs=[
                whole((nodes, width)),
                whole((nodes, head)),
                whole((nodes, head)),
                whole((nodes, 1)),
                pl.BlockSpec((block, head), last),
                pl.BlockSpec((block, head), last),
            ],
            out_specs=(whole((rows, head)), whole((rows, head))),
            scratch_shapes=[
                pltpu.VMEM((rows, head), jnp.bfloat16),
                pltpu.VMEM((rows, head), jnp.float32),
                pltpu.VMEM((rows, head), jnp.float32),
                pltpu.VMEM((rows, head), jnp.float32),
            ],
        ),
        compiler_params=pltpu.CompilerParams(vmem_limit_bytes=56 << 20),
        cost_estimate=pl.CostEstimate(
            flops=6 * rows * half_len * head,
            bytes_accessed=4 * half_len * head,
            transcendentals=rows * half_len,
        ),
        name="attend",
    )(place, lengths, queries, tree_keys, tree_values, parent_row[:, None], keys, values)


def attended(own, came, half):
    rows, head = own.shape
    return pl.pallas_call(
        combine_kernel,
        out_shape=jax.ShapeDtypeStruct((half, rows // 2 // half * head), jnp.bfloat16),
        compiler_params=pltpu.CompilerParams(vmem_limit_bytes=8 << 20),
        name="combine",
    )(own, came)


def local(
    queries,
    tree_keys,
    tree_token_values,
    cache_keys,
    cached_value_rows,
    lengths,
    parents,
    residual,
    out_weight,
    norm_gain,
    gate_weight,
    up_weight,
    down_weight,
):
    core = lax.axis_index("core")
    features = norm_gain.shape[0] * 8
    core, y, zl, zh, x = [lax.axis_index(name) for name in ("core", "y", "zl", "zh", "x")]
    odd = ((y & 1) ^ (x >> 1)) == 1
    swap = (zh ^ (y >> 1)) == 1
    own_first = core == 0
    even = (zl & 1) == 0
    turned_x, turned_zh = turn(x) == 1, zh == 1
    places = [x ^ mask for mask in range(4)]
    odd, swap, own_first, even, turned_x, turned_zh, *places, queries = lax.optimization_barrier(
        (odd, swap, own_first, even, turned_x, turned_zh, *places, queries)
    )
    columns = [over_y(out_weight, mask) for mask in (1, 3, 2)]
    other_gate = over_core(gate_weight)
    other_up = over_core(up_weight)
    length = lax.dynamic_index_in_dim(lengths, lax.axis_index(REQ), keepdims=False)
    parts = attended_parts(
        queries[0],
        tree_keys[0],
        tree_token_values[0],
        cache_keys[0, 0],
        cached_value_rows[0, 0],
        lengths,
        parents[0],
    )
    own, came, near1, near3, other0 = lax.optimization_barrier(
        (parts[0], over_core(parts[1]), *columns[:2], over_core(out_weight))
    )
    attention = attended(own, came, queries.shape[1] // 2)
    attention, other1, other3 = lax.optimization_barrier(
        (attention, over_core(near1), over_core(near3))
    )
    tokens = attention.shape[0]

    rows = from_all_zl(attention, turned_x)
    rows, farthest = lax.optimization_barrier((rows, columns[2]))
    out_weight = jnp.concatenate([out_weight, farthest, near1, near3], axis=1)
    other_out = jnp.concatenate([other0, over_core(farthest), other1, other3], axis=1)
    rows, *weights = lax.optimization_barrier(
        (rows, gate_weight, up_weight, down_weight)
    )
    other_gate, other_up, other_down = [over_core(weight) for weight in weights]

    def classes(products):
        half = products.shape[1] // 2
        a, b = products[:, :half], products[:, half:]
        return jnp.where(odd, b, a), jnp.where(odd, a, b)

    half = 2 * tokens
    mine_stay, mine_away = classes(dot(rows, out_weight))
    theirs = dot(rows, other_out)
    mine_away, theirs_away = lax.optimization_barrier((mine_away, theirs[half:]))
    mine_came, theirs_came = over_x(mine_away, 3), over_x(theirs_away, 1)
    mine = mine_stay + mine_came
    mine_came = over_x(mine[half:], 1)
    theirs_stay, theirs_away = classes(theirs[:half] + theirs_came)
    theirs_came = over_x(theirs_away, 3)
    mine = mine[:half] + mine_came
    theirs = theirs_stay + theirs_came
    mine, theirs, other_gate, other_up, other_down = lax.optimization_barrier(
        (mine, theirs, other_gate, other_up, other_down)
    )
    width = mine.shape[1] // 2

    def item(part, step):
        near, far = [
            jnp.concatenate([a[step * tokens : (step + 1) * tokens, k * width : (k + 1) * width] for a in (mine, theirs)], axis=1)
            for k in (part, 1 - part)
        ]
        return jnp.where(swap, far, near)

    came = [sent(item(*divmod(place, 2)), home_target(place)) for place in range(4)]
    sides = []
    for step in range(2):
        total = came[step] + came[2 + step]
        a, b = total[:, :width], total[:, width:]
        sides.append(
            jnp.concatenate([jnp.where(own_first, a, b), jnp.where(own_first, b, a)], axis=1)
        )
    projected = jnp.concatenate(
        [jnp.where(even, sides[0], sides[1]), jnp.where(even, sides[1], sides[0])], axis=1
    )
    state = residual + projected

    squares = jnp.broadcast_to(jnp.sum(state * state, axis=1), (8, 1, tokens))
    squares = lax.all_to_all(squares, KVH, 0, 0, tiled=True)
    squares = sum([squares[k, 0] for k in range(1, 8)], squares[0, 0])
    normed = (state * lax.rsqrt(squares / features + EPSILON)[:, None] * norm_gain).astype(
        jnp.bfloat16
    )

    first, second = summed_over_x(
        from_all_y(from_all_zl(normed, turned_zh), places), [gate_weight, up_weight], [other_gate, other_up], jnp.bfloat16
    )
    half = 2 * tokens

    ours = first + second
    came = together(over_zh, [s[half:].astype(jnp.bfloat16) for s in ours])
    gate1, up1, gate2, up2 = [s[:half] + g for s, g in zip(ours, came)]
    active = [
        (jax.nn.silu(gate) * up).astype(jnp.bfloat16) for gate, up in ((gate1, up1), (gate2, up2))
    ]

    one, two = [
        jnp.concatenate([a, b]) for a, b in zip(active, together(over_zh, active))
    ]
    one3, two1 = over_x(one, 3), over_x(two, 1)
    one12 = over_x(jnp.concatenate([one, one3]), 1)
    two32 = over_x(jnp.concatenate([two, two1]), 3)
    block = one.shape[0]
    parts = {
        0: (one, two),
        3: (one3, two32[:block]),
        1: (one12[:block], two1),
        2: (one12[block:], two32[block:]),
    }
    down = jnp.stack(
        [
            (dot(a, down_weight) + dot(b, other_down)).astype(jnp.bfloat16)
            for a, b in (parts[mask] for mask in range(4))
        ]
    )
    block = [lax.dynamic_index_in_dim(down, place, keepdims=False) for place in places]
    line = block[0].astype(jnp.float32)
    for mask in (2, 1, 3):
        line = line + over_y(block[mask], mask).astype(jnp.float32)
    line = halves_in_order(line, turned_zh)
    result = state + line[:tokens]
    for mask in (2, 3, 1):
        piece = line[mask * tokens : (mask + 1) * tokens].astype(jnp.bfloat16)
        result = result + over_zl(piece, mask).astype(jnp.float32)
    return result


def solution(mesh):
    split = Mesh(mesh.devices.reshape(4, 4, 2, 4, 2), ("y", "zl", "zh", "x", "core"))
    all_rows = (*REQ, "core")
    in_specs = (
        P(REQ, None, KVH),
        P(REQ, None, KVH),
        P(REQ, None, KVH),
        P(REQ, KVH, "core", None),
        P(REQ, KVH, "core", None),
        P(),
        P(REQ, None),
        P(all_rows, KVH),
        P(KVH, all_rows),
        P(KVH),
        P(KVH, all_rows),
        P(KVH, all_rows),
        P(all_rows, KVH),
    )
    return jax.shard_map(
        local, mesh=split, in_specs=in_specs, out_specs=P(all_rows, KVH), check_vma=False
    )
```

```python
import math

import jax
import jax.numpy as jnp
from jax import lax
from jax.experimental import pallas as pl
from jax.experimental.pallas import tpu as pltpu
from jax.sharding import Mesh
from jax.sharding import PartitionSpec as P

KB = 2048
REQ = ("y", "zl")
KVH = ("zh", "x")
GRID = ("y", "zl", "zh", "x")
SIZES = (4, 4, 2, 4)
MASKED = -1e30
EPSILON = 1e-05


def sent(array, target):
    pairs = []
    for source in range(128):
        x, zh, zl, y = source % 4, source // 4 % 2, source // 8 % 4, source // 32
        to = target(y, zl, zh, x)
        pairs.append((source, ((to[0] * 4 + to[1]) * 2 + to[2]) * 4 + to[3]))
    return lax.ppermute(array, GRID, pairs)


def over_x(array, mask):
    return lax.ppermute(array, "x", [(i, i ^ mask) for i in range(4)])


def over_zh(array):
    return lax.ppermute(array, "zh", [(0, 1), (1, 0)])


def over_core(array):
    return lax.ppermute(array, "core", [(0, 1), (1, 0)])


def turn(x):
    return (x >> 1) ^ (x & 1)


def home_target(place):
    part, step = divmod(place, 2)
    return lambda y, zl, zh, x: (
        y,
        2 * (turn(x) ^ (zl >> 1)) + ((zl & 1) ^ step),
        zh ^ part,
        2 * (x >> 1) + (zl >> 1),
    )


def over_y(array, mask):
    return lax.ppermute(array, "y", [(i, i ^ mask) for i in range(4)])


def over_zl(array, mask):
    return lax.ppermute(array, "zl", [(i, i ^ mask) for i in range(4)])


def halves_in_order(array, turned):
    half = array.shape[0] // 2
    return jnp.where(turned, jnp.concatenate([array[half:], array[:half]]), array)


def from_all_zl(rows, turned):
    return halves_in_order(
        jnp.concatenate([rows] + [over_zl(rows, mask) for mask in (1, 2, 3)]), turned
    )


def from_all_y(line, places):
    blocks = jnp.stack([line] + [over_y(line, mask) for mask in (1, 2, 3)])
    return [lax.dynamic_index_in_dim(blocks, place, keepdims=False) for place in places]


def together(move, arrays, *how):
    joined = move(jnp.concatenate(arrays, axis=1), *how)
    cuts = [sum(a.shape[1] for a in arrays[: k + 1]) for k in range(len(arrays) - 1)]
    return jnp.split(joined, cuts, axis=1)


def dot(a, b):
    return jnp.dot(a, b, preferred_element_type=jnp.float32)


def summed_over_x(blocks, first, second):
    pair = lambda a, b: jnp.concatenate([blocks[a], blocks[b]])
    half = blocks[0].shape[0]
    away = dot(pair(1, 2), first), dot(pair(3, 2), second)
    away = lax.optimization_barrier(tuple(a.astype(jnp.bfloat16) for a in away))
    came = over_x(away[0], 1), over_x(away[1], 3)
    sums = dot(pair(0, 3), first) + came[0], dot(pair(0, 1), second) + came[1]
    last = [over_x(a[half:].astype(jnp.bfloat16), mask) for a, mask in zip(sums, (3, 1))]
    return [a[:half] + g for a, g in zip(sums, last)]


def live_positions(place, lengths, half_len):
    return jnp.clip(lengths[place[0]] - place[1] * half_len, 0, half_len)


def attend_kernel(
    place, lengths, queries, tree_keys, tree_values, parents, keys, values, own, other, rows, top, total, mix
):
    step, core = pl.program_id(0), place[1]
    nodes, width = queries.shape
    block, head = keys.shape
    live = live_positions(place, lengths, block * pl.num_programs(0))
    heads = width // head
    scale = head**-0.5 * math.log2(math.e)

    def scored(key_block):
        return scale * lax.dot_general(
            rows[...], key_block, (((1,), (1,)), ((), ())), preferred_element_type=jnp.float32
        )

    def mixed(weights, value_block):
        high = weights.astype(jnp.bfloat16)
        low = (weights - high.astype(jnp.float32)).astype(jnp.bfloat16)
        return dot(high, value_block) + dot(low, value_block)

    @pl.when(step == 0)
    def _():
        for j in range(heads):
            rows[j * nodes : (j + 1) * nodes, :] = queries[:, j * head : (j + 1) * head]

        @pl.when(core == 0)
        def _():
            places = lax.broadcasted_iota(jnp.int32, (nodes, nodes), 1)
            level = lax.broadcasted_iota(jnp.int32, (nodes, nodes), 0)
            self_only = jnp.where(places == level, 1.0, 0.0)
            below = jnp.where(parents[...] == level, 1.0, self_only)
            for _ in range((nodes - 1).bit_length()):
                below = jnp.minimum(dot(below.astype(jnp.bfloat16), below.astype(jnp.bfloat16)), 1.0)
            reach = lax.dot_general(
                below.astype(jnp.bfloat16),
                self_only.astype(jnp.bfloat16),
                (((0,), (0,)), ((), ())),
                preferred_element_type=jnp.float32,
            )
            reach = jnp.concatenate([reach] * heads)
            scores = jnp.where(reach > 0.5, scored(tree_keys[...]), MASKED)
            highest = jnp.max(scores, axis=1, keepdims=True)
            weights = jnp.exp2(scores - highest)
            top[...] = jnp.broadcast_to(highest, top.shape)
            total[...] = jnp.broadcast_to(jnp.sum(weights, axis=1, keepdims=True), total.shape)
            mix[...] = mixed(weights, tree_values[...])

        @pl.when(core != 0)
        def _():
            top[...] = jnp.full(top.shape, MASKED, jnp.float32)
            total[...] = jnp.zeros(total.shape, jnp.float32)
            mix[...] = jnp.zeros(mix.shape, jnp.float32)

    def absorb(scores):
        before = top[:, :1]
        highest = jnp.maximum(before, jnp.max(scores, axis=1, keepdims=True))
        weights = jnp.exp2(scores - highest)
        factor = jnp.exp2(before - highest)
        top[...] = jnp.broadcast_to(highest, top.shape)
        total[...] = total[...] * factor + jnp.sum(weights, axis=1, keepdims=True)
        mix[...] = mix[...] * factor + mixed(weights, values[...])

    @pl.when((step + 1) * block <= live)
    def _():
        absorb(scored(keys[...]))

    @pl.when((step * block < live) & (live < (step + 1) * block))
    def _():
        positions = step * block + lax.broadcasted_iota(jnp.int32, (rows.shape[0], block), 1)
        absorb(jnp.where(positions < live, scored(keys[...]), MASKED))

    @pl.when(step == pl.num_programs(0) - 1)
    def _():
        half = nodes // 2
        count = heads * half
        first = lax.broadcasted_iota(jnp.int32, (half, head), 1) < head // 2
        for side, out in ((core, own), (1 - core, other)):
            for j in range(heads):
                here = pl.ds(pl.multiple_of(j * nodes + side * half, half), half)
                out[j * half : (j + 1) * half, :] = mix[here, :]
                out[count + j * half : count + (j + 1) * half, :] = jnp.where(
                    first, top[here, :], total[here, :]
                )


def combine_kernel(own, came, out):
    half = out.shape[0]
    count, head = own.shape[0] // 2, own.shape[1]
    for j in range(count // half):
        here = slice(j * half, (j + 1) * half)
        numbers = slice(count + j * half, count + (j + 1) * half)
        top1, total1 = own[numbers, :1], own[numbers, head - 1 :]
        top2, total2 = came[numbers, :1], came[numbers, head - 1 :]
        highest = jnp.maximum(top1, top2)
        factor1, factor2 = jnp.exp2(top1 - highest), jnp.exp2(top2 - highest)
        total = total1 * factor1 + total2 * factor2
        value = (own[here, :] * factor1 + came[here, :] * factor2) / total
        out[:, j * head : (j + 1) * head] = value.astype(out.dtype)


def attended_parts(queries, tree_keys, tree_values, keys, values, lengths, parents):
    nodes, width = queries.shape
    half_len, head = keys.shape
    rows = width // head * nodes
    block = min(KB, half_len)
    place = jnp.stack([lax.axis_index(REQ), lax.axis_index("core")]).astype(jnp.int32)
    whole = lambda shape: pl.BlockSpec(shape, lambda i, place, lengths: (0, 0))

    def last(i, place, lengths):
        live = live_positions(place, lengths, half_len)
        return jnp.minimum(i, jnp.maximum(live - 1, 0) // block), 0

    side = jax.ShapeDtypeStruct((rows, head), jnp.float32)
    return pl.pallas_call(
        attend_kernel,
        out_shape=(side, side),
        grid_spec=pltpu.PrefetchScalarGridSpec(
            num_scalar_prefetch=2,
            grid=(half_len // block,),
            in_specs=[
                whole((nodes, width)),
                whole((nodes, head)),
                whole((nodes, head)),
                whole((1, nodes)),
                pl.BlockSpec((block, head), last),
                pl.BlockSpec((block, head), last),
            ],
            out_specs=(whole((rows, head)), whole((rows, head))),
            scratch_shapes=[
                pltpu.VMEM((rows, head), jnp.bfloat16),
                pltpu.VMEM((rows, head), jnp.float32),
                pltpu.VMEM((rows, head), jnp.float32),
                pltpu.VMEM((rows, head), jnp.float32),
            ],
        ),
        compiler_params=pltpu.CompilerParams(vmem_limit_bytes=56 << 20),
        cost_estimate=pl.CostEstimate(
            flops=6 * rows * half_len * head,
            bytes_accessed=4 * half_len * head,
            transcendentals=rows * half_len,
        ),
        name="attend",
    )(place, lengths, queries, tree_keys, tree_values, parents, keys, values)


def attended(own, came, half):
    rows, head = own.shape
    return pl.pallas_call(
        combine_kernel,
        out_shape=jax.ShapeDtypeStruct((half, rows // 2 // half * head), jnp.bfloat16),
        compiler_params=pltpu.CompilerParams(vmem_limit_bytes=8 << 20),
        name="combine",
    )(own, came)


def local(
    queries,
    tree_keys,
    tree_token_values,
    cache_keys,
    cached_value_rows,
    lengths,
    parents,
    residual,
    out_weight,
    norm_gain,
    gate_weight,
    up_weight,
    down_weight,
):
    core = lax.axis_index("core")
    features = norm_gain.shape[0] * 8
    core, y, zl, zh, x = [lax.axis_index(name) for name in ("core", "y", "zl", "zh", "x")]
    odd = ((y & 1) ^ (x >> 1)) == 1
    swap = (zh ^ (y >> 1)) == 1
    own_first = core == 0
    even = (zl & 1) == 0
    turned_x, turned_zh = turn(x) == 1, zh == 1
    places = [x ^ mask for mask in range(4)]
    odd, swap, own_first, even, turned_x, turned_zh, *places, queries = lax.optimization_barrier(
        (odd, swap, own_first, even, turned_x, turned_zh, *places, queries)
    )
    columns = [over_y(out_weight, 1), over_y(out_weight, 3)]
    other_gate = over_core(gate_weight)
    other_up = over_core(up_weight)
    length = lax.dynamic_index_in_dim(lengths, lax.axis_index(REQ), keepdims=False)
    parts = attended_parts(
        queries[0],
        tree_keys[0],
        tree_token_values[0],
        cache_keys[0, 0],
        cached_value_rows[0, 0],
        lengths,
        parents,
    )
    own, came, near1, near3, other0 = lax.optimization_barrier(
        (parts[0], over_core(parts[1]), *columns, over_core(out_weight))
    )
    half = out_weight.shape[0] // 2
    far = over_y(near1[:half], 3), over_y(near3[half:], 1)
    attention = attended(own, came, queries.shape[1] // 2)
    attention, other1, other3, *weights = lax.optimization_barrier(
        (attention, over_core(near1), over_core(near3), gate_weight, up_weight)
    )
    both_weight = jnp.concatenate(weights, axis=1)
    tokens = attention.shape[0]

    rows = from_all_zl(attention, turned_x)
    rows, *far = lax.optimization_barrier((rows, *far))
    farthest = jnp.concatenate(far)
    out_weight = jnp.concatenate([out_weight, farthest, near1, near3], axis=1)
    other_out = jnp.concatenate([other0, over_core(farthest), other1, other3], axis=1)
    rows, *weights = lax.optimization_barrier(
        (rows, both_weight, down_weight)
    )
    both_weight = weights[0]
    other_both, other_down = [over_core(weight) for weight in weights]

    def classes(products):
        half = products.shape[1] // 2
        a, b = products[:, :half], products[:, half:]
        return jnp.where(odd, b, a), jnp.where(odd, a, b)

    half = 2 * tokens
    mine_stay, mine_away = classes(dot(rows, out_weight))
    theirs = dot(rows, other_out)
    mine_away, theirs_away = lax.optimization_barrier((mine_away, theirs[half:]))
    mine_came, theirs_came = over_x(mine_away, 3), over_x(theirs_away, 1)
    mine = mine_stay + mine_came
    mine_came = over_x(mine[half:], 1)
    theirs_stay, theirs_away = classes(theirs[:half] + theirs_came)
    theirs_came = over_x(theirs_away, 3)
    mine = mine[:half] + mine_came
    theirs = theirs_stay + theirs_came
    mine, theirs, other_both, other_down = lax.optimization_barrier(
        (mine, theirs, other_both, other_down)
    )
    width = mine.shape[1] // 2

    def item(part, step):
        near, far = [
            jnp.concatenate([a[step * tokens : (step + 1) * tokens, k * width : (k + 1) * width] for a in (mine, theirs)], axis=1)
            for k in (part, 1 - part)
        ]
        return jnp.where(swap, far, near)

    came = [sent(item(*divmod(place, 2)), home_target(place)) for place in range(4)]
    sides = []
    for step in range(2):
        total = came[step] + came[2 + step]
        a, b = total[:, :width], total[:, width:]
        sides.append(
            jnp.concatenate([jnp.where(own_first, a, b), jnp.where(own_first, b, a)], axis=1)
        )
    projected = jnp.concatenate(
        [jnp.where(even, sides[0], sides[1]), jnp.where(even, sides[1], sides[0])], axis=1
    )
    state = residual + projected

    squares = jnp.broadcast_to(jnp.sum(state * state, axis=1), (8, 1, tokens))
    squares = lax.all_to_all(squares, KVH, 0, 0, tiled=True)
    squares = sum([squares[k, 0] for k in range(1, 8)], squares[0, 0])
    normed = (state * lax.rsqrt(squares / features + EPSILON)[:, None] * norm_gain).astype(
        jnp.bfloat16
    )

    ours = summed_over_x(
        from_all_y(from_all_zl(normed, turned_zh), places), both_weight, other_both
    )
    half = 2 * tokens
    came = together(over_zh, [s[half:].astype(jnp.bfloat16) for s in ours])
    active = []
    for own, more in zip(ours, came):
        gate, up = jnp.split(own[:half] + more, 2, axis=1)
        active.append((jax.nn.silu(gate) * up).astype(jnp.bfloat16))

    one, two = [
        jnp.concatenate([a, b]) for a, b in zip(active, together(over_zh, active))
    ]
    one3, two1 = over_x(one, 3), over_x(two, 1)
    one12 = over_x(jnp.concatenate([one, one3]), 1)
    two32 = over_x(jnp.concatenate([two, two1]), 3)
    block = one.shape[0]
    parts = {
        0: (one, two),
        3: (one3, two32[:block]),
        1: (one12[:block], two1),
        2: (one12[block:], two32[block:]),
    }
    down = jnp.stack(
        [
            (dot(a, down_weight) + dot(b, other_down)).astype(jnp.bfloat16)
            for a, b in (parts[mask] for mask in range(4))
        ]
    )
    block = [lax.dynamic_index_in_dim(down, place, keepdims=False) for place in places]
    line = block[0].astype(jnp.float32)
    for mask in (2, 1, 3):
        line = line + over_y(block[mask], mask).astype(jnp.float32)
    line = halves_in_order(line, turned_zh)
    result = state + line[:tokens]
    for mask in (2, 3, 1):
        piece = line[mask * tokens : (mask + 1) * tokens].astype(jnp.bfloat16)
        result = result + over_zl(piece, mask).astype(jnp.float32)
    return result


def solution(mesh):
    split = Mesh(mesh.devices.reshape(4, 4, 2, 4, 2), ("y", "zl", "zh", "x", "core"))
    all_rows = (*REQ, "core")
    in_specs = (
        P(REQ, None, KVH),
        P(REQ, None, KVH),
        P(REQ, None, KVH),
        P(REQ, KVH, "core", None),
        P(REQ, KVH, "core", None),
        P(),
        P(REQ, None),
        P(all_rows, KVH),
        P(KVH, all_rows),
        P(KVH),
        P(KVH, all_rows),
        P(KVH, all_rows),
        P(all_rows, KVH),
    )
    return jax.shard_map(
        local, mesh=split, in_specs=in_specs, out_specs=P(all_rows, KVH), check_vma=False
    )
```

```python
import math

import jax
import jax.numpy as jnp
from jax import lax
from jax.experimental import pallas as pl
from jax.experimental.pallas import tpu as pltpu
from jax.sharding import Mesh
from jax.sharding import PartitionSpec as P

KB = 2048
REQ = ("y", "zl")
KVH = ("zh", "x")
GRID = ("y", "zl", "zh", "x")
SIZES = (4, 4, 2, 4)
MASKED = -1e30
EPSILON = 1e-05


def sent(array, target):
    pairs = []
    for source in range(128):
        x, zh, zl, y = source % 4, source // 4 % 2, source // 8 % 4, source // 32
        to = target(y, zl, zh, x)
        pairs.append((source, ((to[0] * 4 + to[1]) * 2 + to[2]) * 4 + to[3]))
    return lax.ppermute(array, GRID, pairs)


def over_x(array, mask):
    return lax.ppermute(array, "x", [(i, i ^ mask) for i in range(4)])


def over_zh(array):
    return lax.ppermute(array, "zh", [(0, 1), (1, 0)])


def over_core(array):
    return lax.ppermute(array, "core", [(0, 1), (1, 0)])


def turn(x):
    return (x >> 1) ^ (x & 1)


def home_target(place):
    part, step = divmod(place, 2)
    return lambda y, zl, zh, x: (
        y,
        2 * (turn(x) ^ (zl >> 1)) + ((zl & 1) ^ step),
        zh ^ part,
        2 * (x >> 1) + (zl >> 1),
    )


def over_y(array, mask):
    return lax.ppermute(array, "y", [(i, i ^ mask) for i in range(4)])


def over_zl(array, mask):
    return lax.ppermute(array, "zl", [(i, i ^ mask) for i in range(4)])


def halves_in_order(array, turned):
    half = array.shape[0] // 2
    return jnp.where(turned, jnp.concatenate([array[half:], array[:half]]), array)


def from_all_zl(rows, turned):
    return halves_in_order(
        jnp.concatenate([rows] + [over_zl(rows, mask) for mask in (1, 2, 3)]), turned
    )


def block_at(blocks, place):
    return lax.dynamic_index_in_dim(
        blocks, place, keepdims=False, allow_negative_indices=False
    )


def from_all_y(line, places):
    blocks = jnp.stack([line] + [over_y(line, mask) for mask in (1, 2, 3)])
    return [block_at(blocks, place) for place in places]


def together(move, arrays, *how):
    joined = move(jnp.concatenate(arrays, axis=1), *how)
    cuts = [sum(a.shape[1] for a in arrays[: k + 1]) for k in range(len(arrays) - 1)]
    return jnp.split(joined, cuts, axis=1)


def dot(a, b):
    return jnp.dot(a, b, preferred_element_type=jnp.float32)


def summed_over_x(blocks, first, second):
    pair = lambda a, b: jnp.concatenate([blocks[a], blocks[b]])
    half = blocks[0].shape[0]
    away = dot(pair(1, 2), first), dot(pair(3, 2), second)
    away = lax.optimization_barrier(tuple(a.astype(jnp.bfloat16) for a in away))
    came = over_x(away[0], 1), over_x(away[1], 3)
    sums = dot(pair(0, 3), first) + came[0], dot(pair(0, 1), second) + came[1]
    last = [over_x(a[half:].astype(jnp.bfloat16), mask) for a, mask in zip(sums, (3, 1))]
    return [a[:half] + g for a, g in zip(sums, last)]


def live_positions(place, lengths, half_len):
    return jnp.clip(lengths[place[0]] - place[1] * half_len, 0, half_len)


def attend_kernel(
    place, lengths, queries, tree_keys, tree_values, parents, keys, values, own, other, rows, top, total, mix
):
    step, core = pl.program_id(0), place[1]
    nodes, width = queries.shape
    block, head = keys.shape
    live = live_positions(place, lengths, block * pl.num_programs(0))
    heads = width // head
    scale = head**-0.5 * math.log2(math.e)

    def scored(key_block):
        return scale * lax.dot_general(
            rows[...], key_block, (((1,), (1,)), ((), ())), preferred_element_type=jnp.float32
        )

    def mixed(weights, value_block):
        high = weights.astype(jnp.bfloat16)
        low = (weights - high.astype(jnp.float32)).astype(jnp.bfloat16)
        return dot(high, value_block) + dot(low, value_block)

    @pl.when(step == 0)
    def _():
        for j in range(heads):
            rows[j * nodes : (j + 1) * nodes, :] = queries[:, j * head : (j + 1) * head]

        @pl.when(core == 0)
        def _():
            places = lax.broadcasted_iota(jnp.int32, (nodes, nodes), 1)
            level = lax.broadcasted_iota(jnp.int32, (nodes, nodes), 0)
            self_only = jnp.where(places == level, 1.0, 0.0)
            below = jnp.where(parents[...] == level, 1.0, self_only)
            for _ in range((nodes - 1).bit_length()):
                below = jnp.minimum(dot(below.astype(jnp.bfloat16), below.astype(jnp.bfloat16)), 1.0)
            reach = lax.dot_general(
                below.astype(jnp.bfloat16),
                self_only.astype(jnp.bfloat16),
                (((0,), (0,)), ((), ())),
                preferred_element_type=jnp.float32,
            )
            reach = jnp.concatenate([reach] * heads)
            scores = jnp.where(reach > 0.5, scored(tree_keys[...]), MASKED)
            highest = jnp.max(scores, axis=1, keepdims=True)
            weights = jnp.exp2(scores - highest)
            top[...] = jnp.broadcast_to(highest, top.shape)
            total[...] = jnp.broadcast_to(jnp.sum(weights, axis=1, keepdims=True), total.shape)
            mix[...] = mixed(weights, tree_values[...])

        @pl.when(core != 0)
        def _():
            top[...] = jnp.full(top.shape, MASKED, jnp.float32)
            total[...] = jnp.zeros(total.shape, jnp.float32)
            mix[...] = jnp.zeros(mix.shape, jnp.float32)

    def absorb(scores):
        before = top[:, :1]
        highest = jnp.maximum(before, jnp.max(scores, axis=1, keepdims=True))
        weights = jnp.exp2(scores - highest)
        factor = jnp.exp2(before - highest)
        top[...] = jnp.broadcast_to(highest, top.shape)
        total[...] = total[...] * factor + jnp.sum(weights, axis=1, keepdims=True)
        mix[...] = mix[...] * factor + mixed(weights, values[...])

    @pl.when((step + 1) * block <= live)
    def _():
        absorb(scored(keys[...]))

    @pl.when((step * block < live) & (live < (step + 1) * block))
    def _():
        positions = step * block + lax.broadcasted_iota(jnp.int32, (rows.shape[0], block), 1)
        absorb(jnp.where(positions < live, scored(keys[...]), MASKED))

    @pl.when(step == pl.num_programs(0) - 1)
    def _():
        half = nodes // 2
        count = heads * half
        first = lax.broadcasted_iota(jnp.int32, (half, head), 1) < head // 2
        for side, out in ((core, own), (1 - core, other)):
            for j in range(heads):
                here = pl.ds(pl.multiple_of(j * nodes + side * half, half), half)
                out[j * half : (j + 1) * half, :] = mix[here, :]
                out[count + j * half : count + (j + 1) * half, :] = jnp.where(
                    first, top[here, :], total[here, :]
                )


def combine_kernel(own, came, out):
    half = out.shape[0]
    count, head = own.shape[0] // 2, own.shape[1]
    for j in range(count // half):
        here = slice(j * half, (j + 1) * half)
        numbers = slice(count + j * half, count + (j + 1) * half)
        top1, total1 = own[numbers, :1], own[numbers, head - 1 :]
        top2, total2 = came[numbers, :1], came[numbers, head - 1 :]
        highest = jnp.maximum(top1, top2)
        factor1, factor2 = jnp.exp2(top1 - highest), jnp.exp2(top2 - highest)
        total = total1 * factor1 + total2 * factor2
        value = (own[here, :] * factor1 + came[here, :] * factor2) / total
        out[:, j * head : (j + 1) * head] = value.astype(out.dtype)


def attended_parts(queries, tree_keys, tree_values, keys, values, lengths, parents):
    nodes, width = queries.shape
    half_len, head = keys.shape
    rows = width // head * nodes
    block = min(KB, half_len)
    place = jnp.stack([lax.axis_index(REQ), lax.axis_index("core")]).astype(jnp.int32)
    whole = lambda shape: pl.BlockSpec(shape, lambda i, place, lengths: (0, 0))

    def last(i, place, lengths):
        live = live_positions(place, lengths, half_len)
        return jnp.minimum(i, jnp.maximum(live - 1, 0) // block), 0

    side = jax.ShapeDtypeStruct((rows, head), jnp.float32)
    return pl.pallas_call(
        attend_kernel,
        out_shape=(side, side),
        grid_spec=pltpu.PrefetchScalarGridSpec(
            num_scalar_prefetch=2,
            grid=(half_len // block,),
            in_specs=[
                whole((nodes, width)),
                whole((nodes, head)),
                whole((nodes, head)),
                whole((1, nodes)),
                pl.BlockSpec((block, head), last),
                pl.BlockSpec((block, head), last),
            ],
            out_specs=(whole((rows, head)), whole((rows, head))),
            scratch_shapes=[
                pltpu.VMEM((rows, head), jnp.bfloat16),
                pltpu.VMEM((rows, head), jnp.float32),
                pltpu.VMEM((rows, head), jnp.float32),
                pltpu.VMEM((rows, head), jnp.float32),
            ],
        ),
        compiler_params=pltpu.CompilerParams(vmem_limit_bytes=56 << 20),
        cost_estimate=pl.CostEstimate(
            flops=6 * rows * half_len * head,
            bytes_accessed=4 * half_len * head,
            transcendentals=rows * half_len,
        ),
        name="attend",
    )(place, lengths, queries, tree_keys, tree_values, parents, keys, values)


def attended(own, came, half):
    rows, head = own.shape
    return pl.pallas_call(
        combine_kernel,
        out_shape=jax.ShapeDtypeStruct((half, rows // 2 // half * head), jnp.bfloat16),
        compiler_params=pltpu.CompilerParams(vmem_limit_bytes=8 << 20),
        name="combine",
    )(own, came)


def local(
    queries,
    tree_keys,
    tree_token_values,
    cache_keys,
    cached_value_rows,
    lengths,
    parents,
    residual,
    out_weight,
    norm_gain,
    gate_weight,
    up_weight,
    down_weight,
):
    core = lax.axis_index("core")
    features = norm_gain.shape[0] * 8
    core, y, zl, zh, x = [lax.axis_index(name) for name in ("core", "y", "zl", "zh", "x")]
    odd = ((y & 1) ^ (x >> 1)) == 1
    swap = (zh ^ (y >> 1)) == 1
    own_first = core == 0
    even = (zl & 1) == 0
    turned_x, turned_zh = turn(x) == 1, zh == 1
    places = [x ^ mask for mask in range(4)]
    odd, swap, own_first, even, turned_x, turned_zh, *places, queries = lax.optimization_barrier(
        (odd, swap, own_first, even, turned_x, turned_zh, *places, queries)
    )
    columns = [over_y(out_weight, 1), over_y(out_weight, 3)]
    other_gate = over_core(gate_weight)
    other_up = over_core(up_weight)
    length = lax.dynamic_index_in_dim(lengths, lax.axis_index(REQ), keepdims=False)
    parts = attended_parts(
        queries[0],
        tree_keys[0],
        tree_token_values[0],
        cache_keys[0, 0],
        cached_value_rows[0, 0],
        lengths,
        parents,
    )
    own, came, near1, near3, other0 = lax.optimization_barrier(
        (parts[0], over_core(parts[1]), *columns, over_core(out_weight))
    )
    half = out_weight.shape[0] // 2
    far = over_y(near1[:half], 3), over_y(near3[half:], 1)
    attention = attended(own, came, queries.shape[1] // 2)
    attention, other1, other3, *weights = lax.optimization_barrier(
        (attention, over_core(near1), over_core(near3), gate_weight, up_weight)
    )
    both_weight = jnp.concatenate(weights, axis=1)
    tokens = attention.shape[0]

    rows = from_all_zl(attention, turned_x)
    rows, *far = lax.optimization_barrier((rows, *far))
    farthest = jnp.concatenate(far)
    out_weight = jnp.concatenate([out_weight, farthest, near1, near3], axis=1)
    rows, other_far, *weights = lax.optimization_barrier(
        (rows, over_core(farthest), both_weight, down_weight)
    )
    other_out = jnp.concatenate([other0, other_far, other1, other3], axis=1)
    both_weight = weights[0]
    other_both, other_down = [over_core(weight) for weight in weights]

    def classes(products):
        half = products.shape[1] // 2
        a, b = products[:, :half], products[:, half:]
        return jnp.where(odd, b, a), jnp.where(odd, a, b)

    half = 2 * tokens
    mine_stay, mine_away = classes(dot(rows, out_weight))
    theirs = dot(rows, other_out)
    mine_away, theirs_away = lax.optimization_barrier((mine_away, theirs[half:]))
    mine_came, theirs_came = over_x(mine_away, 3), over_x(theirs_away, 1)
    mine = mine_stay + mine_came
    mine_came = over_x(mine[half:], 1)
    theirs_stay, theirs_away = classes(theirs[:half] + theirs_came)
    theirs_came = over_x(theirs_away, 3)
    mine = mine[:half] + mine_came
    theirs = theirs_stay + theirs_came
    mine, theirs, other_both, other_down = lax.optimization_barrier(
        (mine, theirs, other_both, other_down)
    )
    width = mine.shape[1] // 2

    def item(part, step):
        near, far = [
            jnp.concatenate([a[step * tokens : (step + 1) * tokens, k * width : (k + 1) * width] for a in (mine, theirs)], axis=1)
            for k in (part, 1 - part)
        ]
        return jnp.where(swap, far, near)

    came = [sent(item(*divmod(place, 2)), home_target(place)) for place in range(4)]
    sides = []
    for step in range(2):
        total = came[step] + came[2 + step]
        a, b = total[:, :width], total[:, width:]
        sides.append(
            jnp.concatenate([jnp.where(own_first, a, b), jnp.where(own_first, b, a)], axis=1)
        )
    projected = jnp.concatenate(
        [jnp.where(even, sides[0], sides[1]), jnp.where(even, sides[1], sides[0])], axis=1
    )
    state = residual + projected

    squares = jnp.broadcast_to(jnp.sum(state * state, axis=1), (8, 1, tokens))
    squares = lax.all_to_all(squares, KVH, 0, 0, tiled=True)
    squares = sum([squares[k, 0] for k in range(1, 8)], squares[0, 0])
    normed = (state * lax.rsqrt(squares / features + EPSILON)[:, None] * norm_gain).astype(
        jnp.bfloat16
    )

    ours = summed_over_x(
        from_all_y(from_all_zl(normed, turned_zh), places), both_weight, other_both
    )
    half = 2 * tokens
    came = together(over_zh, [s[half:].astype(jnp.bfloat16) for s in ours])
    active = []
    for own, more in zip(ours, came):
        gate, up = jnp.split(own[:half] + more, 2, axis=1)
        active.append((jax.nn.silu(gate) * up).astype(jnp.bfloat16))

    one, two = [
        jnp.concatenate([a, b]) for a, b in zip(active, together(over_zh, active))
    ]
    one3, two1 = over_x(one, 3), over_x(two, 1)
    one12 = over_x(jnp.concatenate([one, one3]), 1)
    two32 = over_x(jnp.concatenate([two, two1]), 3)
    block = one.shape[0]
    parts = {
        0: (one, two),
        3: (one3, two32[:block]),
        1: (one12[:block], two1),
        2: (one12[block:], two32[block:]),
    }
    down = jnp.stack(
        [
            (dot(a, down_weight) + dot(b, other_down)).astype(jnp.bfloat16)
            for a, b in (parts[mask] for mask in range(4))
        ]
    )
    block = [block_at(down, place) for place in places]
    line = block[0].astype(jnp.float32)
    for mask in (2, 1, 3):
        line = line + over_y(block[mask], mask).astype(jnp.float32)
    line = halves_in_order(line, turned_zh)
    result = state + line[:tokens]
    for mask in (2, 3, 1):
        piece = line[mask * tokens : (mask + 1) * tokens].astype(jnp.bfloat16)
        result = result + over_zl(piece, mask).astype(jnp.float32)
    return result


def solution(mesh):
    split = Mesh(mesh.devices.reshape(4, 4, 2, 4, 2), ("y", "zl", "zh", "x", "core"))
    all_rows = (*REQ, "core")
    in_specs = (
        P(REQ, None, KVH),
        P(REQ, None, KVH),
        P(REQ, None, KVH),
        P(REQ, KVH, "core", None),
        P(REQ, KVH, "core", None),
        P(),
        P(REQ, None),
        P(all_rows, KVH),
        P(KVH, all_rows),
        P(KVH),
        P(KVH, all_rows),
        P(KVH, all_rows),
        P(all_rows, KVH),
    )
    return jax.shard_map(
        local, mesh=split, in_specs=in_specs, out_specs=P(all_rows, KVH), check_vma=False
    )
```

```python
import math

import jax
import jax.numpy as jnp
from jax import lax
from jax.experimental import pallas as pl
from jax.experimental.pallas import tpu as pltpu
from jax.sharding import Mesh
from jax.sharding import PartitionSpec as P

KB = 2048
REQ = ("y", "zl")
KVH = ("zh", "x")
GRID = ("y", "zl", "zh", "x")
SIZES = (4, 4, 2, 4)
MASKED = -1e30
EPSILON = 1e-05


def sent(array, target):
    pairs = []
    for source in range(128):
        x, zh, zl, y = source % 4, source // 4 % 2, source // 8 % 4, source // 32
        to = target(y, zl, zh, x)
        pairs.append((source, ((to[0] * 4 + to[1]) * 2 + to[2]) * 4 + to[3]))
    return lax.ppermute(array, GRID, pairs)


def over_x(array, mask):
    return lax.ppermute(array, "x", [(i, i ^ mask) for i in range(4)])


def over_zh(array):
    return lax.ppermute(array, "zh", [(0, 1), (1, 0)])


def over_core(array):
    return lax.ppermute(array, "core", [(0, 1), (1, 0)])


def line_target(place):
    part, step = divmod(place, 2)
    return lambda y, zl, zh, x: (y, zl ^ (2 * (part ^ zh) + step), zh, x)


def turn(x):
    return (x >> 1) ^ (x & 1)


def home_target(place):
    part, step = divmod(place, 2)
    return lambda y, zl, zh, x: (
        y,
        2 * (turn(x) ^ (zl >> 1)) + ((zl & 1) ^ step),
        zh ^ part,
        2 * (x >> 1) + (zl >> 1),
    )


def over_y(array, mask):
    return lax.ppermute(array, "y", [(i, i ^ mask) for i in range(4)])


def over_zl(array, mask):
    return lax.ppermute(array, "zl", [(i, i ^ mask) for i in range(4)])


def halves_in_order(array, turned):
    half = array.shape[0] // 2
    return jnp.where(turned, jnp.concatenate([array[half:], array[:half]]), array)


def from_all_zl(rows, turned):
    return halves_in_order(
        jnp.concatenate([rows] + [over_zl(rows, mask) for mask in (1, 2, 3)]), turned
    )


def block_at(blocks, place):
    return lax.dynamic_index_in_dim(
        blocks, place, keepdims=False, allow_negative_indices=False
    )


def from_all_y(line, places):
    blocks = jnp.stack([line] + [over_y(line, mask) for mask in (1, 2, 3)])
    return [block_at(blocks, place) for place in places]


def together(move, arrays, *how):
    joined = move(jnp.concatenate(arrays, axis=1), *how)
    cuts = [sum(a.shape[1] for a in arrays[: k + 1]) for k in range(len(arrays) - 1)]
    return jnp.split(joined, cuts, axis=1)


def dot(a, b):
    return jnp.dot(a, b, preferred_element_type=jnp.float32)


def summed_over_x(blocks, first, second):
    pair = lambda a, b: jnp.concatenate([blocks[a], blocks[b]])
    half = blocks[0].shape[0]
    away = dot(pair(1, 2), first), dot(pair(3, 2), second)
    away = lax.optimization_barrier(tuple(a.astype(jnp.bfloat16) for a in away))
    came = over_x(away[0], 1), over_x(away[1], 3)
    sums = dot(pair(0, 3), first) + came[0], dot(pair(0, 1), second) + came[1]
    last = [over_x(a[half:].astype(jnp.bfloat16), mask) for a, mask in zip(sums, (3, 1))]
    return [a[:half] + g for a, g in zip(sums, last)]


def live_positions(place, lengths, half_len):
    return jnp.clip(lengths[place[0]] - place[1] * half_len, 0, half_len)


def attend_kernel(
    place, lengths, queries, tree_keys, tree_values, parents, keys, values, own, other, rows, top, total, mix
):
    step, core = pl.program_id(0), place[1]
    nodes, width = queries.shape
    block, head = keys.shape
    live = live_positions(place, lengths, block * pl.num_programs(0))
    heads = width // head
    scale = head**-0.5 * math.log2(math.e)

    def scored(key_block):
        return scale * lax.dot_general(
            rows[...], key_block, (((1,), (1,)), ((), ())), preferred_element_type=jnp.float32
        )

    def mixed(weights, value_block):
        high = weights.astype(jnp.bfloat16)
        low = (weights - high.astype(jnp.float32)).astype(jnp.bfloat16)
        return dot(high, value_block) + dot(low, value_block)

    @pl.when(step == 0)
    def _():
        for j in range(heads):
            rows[j * nodes : (j + 1) * nodes, :] = queries[:, j * head : (j + 1) * head]

        @pl.when(core == 0)
        def _():
            places = lax.broadcasted_iota(jnp.int32, (nodes, nodes), 1)
            level = lax.broadcasted_iota(jnp.int32, (nodes, nodes), 0)
            self_only = jnp.where(places == level, 1.0, 0.0)
            below = jnp.where(parents[...] == level, 1.0, self_only)
            for _ in range((nodes - 1).bit_length()):
                below = jnp.minimum(dot(below.astype(jnp.bfloat16), below.astype(jnp.bfloat16)), 1.0)
            reach = lax.dot_general(
                below.astype(jnp.bfloat16),
                self_only.astype(jnp.bfloat16),
                (((0,), (0,)), ((), ())),
                preferred_element_type=jnp.float32,
            )
            reach = jnp.concatenate([reach] * heads)
            scores = jnp.where(reach > 0.5, scored(tree_keys[...]), MASKED)
            highest = jnp.max(scores, axis=1, keepdims=True)
            weights = jnp.exp2(scores - highest)
            top[...] = jnp.broadcast_to(highest, top.shape)
            total[...] = jnp.broadcast_to(jnp.sum(weights, axis=1, keepdims=True), total.shape)
            mix[...] = mixed(weights, tree_values[...])

        @pl.when(core != 0)
        def _():
            top[...] = jnp.full(top.shape, MASKED, jnp.float32)
            total[...] = jnp.zeros(total.shape, jnp.float32)
            mix[...] = jnp.zeros(mix.shape, jnp.float32)

    def absorb(scores):
        before = top[:, :1]
        highest = jnp.maximum(before, jnp.max(scores, axis=1, keepdims=True))
        weights = jnp.exp2(scores - highest)
        factor = jnp.exp2(before - highest)
        top[...] = jnp.broadcast_to(highest, top.shape)
        total[...] = total[...] * factor + jnp.sum(weights, axis=1, keepdims=True)
        mix[...] = mix[...] * factor + mixed(weights, values[...])

    @pl.when((step + 1) * block <= live)
    def _():
        absorb(scored(keys[...]))

    @pl.when((step * block < live) & (live < (step + 1) * block))
    def _():
        positions = step * block + lax.broadcasted_iota(jnp.int32, (rows.shape[0], block), 1)
        absorb(jnp.where(positions < live, scored(keys[...]), MASKED))

    @pl.when(step == pl.num_programs(0) - 1)
    def _():
        half = nodes // 2
        count = heads * half
        first = lax.broadcasted_iota(jnp.int32, (half, head), 1) < head // 2
        for side, out in ((core, own), (1 - core, other)):
            for j in range(heads):
                here = pl.ds(pl.multiple_of(j * nodes + side * half, half), half)
                out[j * half : (j + 1) * half, :] = mix[here, :]
                out[count + j * half : count + (j + 1) * half, :] = jnp.where(
                    first, top[here, :], total[here, :]
                )


def combine_kernel(own, came, out):
    half = out.shape[0]
    count, head = own.shape[0] // 2, own.shape[1]
    for j in range(count // half):
        here = slice(j * half, (j + 1) * half)
        numbers = slice(count + j * half, count + (j + 1) * half)
        top1, total1 = own[numbers, :1], own[numbers, head - 1 :]
        top2, total2 = came[numbers, :1], came[numbers, head - 1 :]
        highest = jnp.maximum(top1, top2)
        factor1, factor2 = jnp.exp2(top1 - highest), jnp.exp2(top2 - highest)
        total = total1 * factor1 + total2 * factor2
        value = (own[here, :] * factor1 + came[here, :] * factor2) / total
        out[:, j * head : (j + 1) * head] = value.astype(out.dtype)


def attended_parts(queries, tree_keys, tree_values, keys, values, lengths, parents):
    nodes, width = queries.shape
    half_len, head = keys.shape
    rows = width // head * nodes
    block = min(KB, half_len)
    place = jnp.stack([lax.axis_index(REQ), lax.axis_index("core")]).astype(jnp.int32)
    whole = lambda shape: pl.BlockSpec(shape, lambda i, place, lengths: (0, 0))

    def last(i, place, lengths):
        live = live_positions(place, lengths, half_len)
        return jnp.minimum(i, jnp.maximum(live - 1, 0) // block), 0

    side = jax.ShapeDtypeStruct((rows, head), jnp.float32)
    return pl.pallas_call(
        attend_kernel,
        out_shape=(side, side),
        grid_spec=pltpu.PrefetchScalarGridSpec(
            num_scalar_prefetch=2,
            grid=(half_len // block,),
            in_specs=[
                whole((nodes, width)),
                whole((nodes, head)),
                whole((nodes, head)),
                whole((1, nodes)),
                pl.BlockSpec((block, head), last),
                pl.BlockSpec((block, head), last),
            ],
            out_specs=(whole((rows, head)), whole((rows, head))),
            scratch_shapes=[
                pltpu.VMEM((rows, head), jnp.bfloat16),
                pltpu.VMEM((rows, head), jnp.float32),
                pltpu.VMEM((rows, head), jnp.float32),
                pltpu.VMEM((rows, head), jnp.float32),
            ],
        ),
        compiler_params=pltpu.CompilerParams(vmem_limit_bytes=56 << 20),
        cost_estimate=pl.CostEstimate(
            flops=6 * rows * half_len * head,
            bytes_accessed=4 * half_len * head,
            transcendentals=rows * half_len,
        ),
        name="attend",
    )(place, lengths, queries, tree_keys, tree_values, parents, keys, values)


def attended(own, came, half):
    rows, head = own.shape
    return pl.pallas_call(
        combine_kernel,
        out_shape=jax.ShapeDtypeStruct((half, rows // 2 // half * head), jnp.bfloat16),
        compiler_params=pltpu.CompilerParams(vmem_limit_bytes=8 << 20),
        name="combine",
    )(own, came)


def local(
    queries,
    tree_keys,
    tree_token_values,
    cache_keys,
    cached_value_rows,
    lengths,
    parents,
    residual,
    out_weight,
    norm_gain,
    gate_weight,
    up_weight,
    down_weight,
):
    core = lax.axis_index("core")
    features = norm_gain.shape[0] * 8
    core, y, zl, zh, x = [lax.axis_index(name) for name in ("core", "y", "zl", "zh", "x")]
    odd = ((y & 1) ^ (x >> 1)) == 1
    swap = (zh ^ (y >> 1)) == 1
    own_first = core == 0
    even = (zl & 1) == 0
    turned_x, turned_zh = turn(x) == 1, zh == 1
    places = [x ^ mask for mask in range(4)]
    odd, swap, own_first, even, turned_x, turned_zh, *places, queries = lax.optimization_barrier(
        (odd, swap, own_first, even, turned_x, turned_zh, *places, queries)
    )
    columns = [over_y(out_weight, 1), over_y(out_weight, 3)]
    other_gate = over_core(gate_weight)
    other_up = over_core(up_weight)
    length = lax.dynamic_index_in_dim(lengths, lax.axis_index(REQ), keepdims=False)
    parts = attended_parts(
        queries[0],
        tree_keys[0],
        tree_token_values[0],
        cache_keys[0, 0],
        cached_value_rows[0, 0],
        lengths,
        parents,
    )
    own, came, near1, near3, other0 = lax.optimization_barrier(
        (parts[0], over_core(parts[1]), *columns, over_core(out_weight))
    )
    half = out_weight.shape[0] // 2
    far = over_y(near1[:half], 3), over_y(near3[half:], 1)
    attention = attended(own, came, queries.shape[1] // 2)
    attention, other1, other3, *weights = lax.optimization_barrier(
        (attention, over_core(near1), over_core(near3), gate_weight, up_weight)
    )
    both_weight = jnp.concatenate(weights, axis=1)
    tokens = attention.shape[0]

    rows = from_all_zl(attention, turned_x)
    rows, *far = lax.optimization_barrier((rows, *far))
    farthest = jnp.concatenate(far)
    out_weight = jnp.concatenate([out_weight, farthest, near1, near3], axis=1)
    rows, other_far, *weights = lax.optimization_barrier(
        (rows, over_core(farthest), both_weight, down_weight)
    )
    other_out = jnp.concatenate([other0, other_far, other1, other3], axis=1)
    both_weight = weights[0]
    other_both, other_down = [over_core(weight) for weight in weights]

    def classes(products):
        half = products.shape[1] // 2
        a, b = products[:, :half], products[:, half:]
        return jnp.where(odd, b, a), jnp.where(odd, a, b)

    half = 2 * tokens
    mine_stay, mine_away = classes(dot(rows, out_weight))
    theirs = dot(rows, other_out)
    mine_away, theirs_away = lax.optimization_barrier((mine_away, theirs[half:]))
    mine_came, theirs_came = over_x(mine_away, 3), over_x(theirs_away, 1)
    mine = mine_stay + mine_came
    mine_came = over_x(mine[half:], 1)
    theirs_stay, theirs_away = classes(theirs[:half] + theirs_came)
    theirs_came = over_x(theirs_away, 3)
    mine = mine[:half] + mine_came
    theirs = theirs_stay + theirs_came
    mine, theirs, other_both, other_down = lax.optimization_barrier(
        (mine, theirs, other_both, other_down)
    )
    width = mine.shape[1] // 2

    def item(part, step):
        near, far = [
            jnp.concatenate([a[step * tokens : (step + 1) * tokens, k * width : (k + 1) * width] for a in (mine, theirs)], axis=1)
            for k in (part, 1 - part)
        ]
        return jnp.where(swap, far, near)

    came = [sent(item(*divmod(place, 2)), home_target(place)) for place in range(4)]
    sides = []
    for step in range(2):
        total = came[step] + came[2 + step]
        a, b = total[:, :width], total[:, width:]
        sides.append(
            jnp.concatenate([jnp.where(own_first, a, b), jnp.where(own_first, b, a)], axis=1)
        )
    projected = jnp.concatenate(
        [jnp.where(even, sides[0], sides[1]), jnp.where(even, sides[1], sides[0])], axis=1
    )
    state = residual + projected

    squares = jnp.broadcast_to(jnp.sum(state * state, axis=1), (8, 1, tokens))
    squares = lax.all_to_all(squares, KVH, 0, 0, tiled=True)
    squares = sum([squares[k, 0] for k in range(1, 8)], squares[0, 0])
    normed = (state * lax.rsqrt(squares / features + EPSILON)[:, None] * norm_gain).astype(
        jnp.bfloat16
    )

    ours = summed_over_x(
        from_all_y(from_all_zl(normed, turned_zh), places), both_weight, other_both
    )
    half = 2 * tokens
    came = together(over_zh, [s[half:].astype(jnp.bfloat16) for s in ours])
    active = []
    for own, more in zip(ours, came):
        gate, up = jnp.split(own[:half] + more, 2, axis=1)
        active.append((jax.nn.silu(gate) * up).astype(jnp.bfloat16))

    one, two = [
        jnp.concatenate([a, b]) for a, b in zip(active, together(over_zh, active))
    ]
    one3, two1 = over_x(one, 3), over_x(two, 1)
    one12 = over_x(jnp.concatenate([one, one3]), 1)
    two32 = over_x(jnp.concatenate([two, two1]), 3)
    block = one.shape[0]
    parts = {
        0: (one, two),
        3: (one3, two32[:block]),
        1: (one12[:block], two1),
        2: (one12[block:], two32[block:]),
    }
    down = jnp.stack(
        [
            (dot(a, down_weight) + dot(b, other_down)).astype(jnp.bfloat16)
            for a, b in (parts[mask] for mask in range(4))
        ]
    )
    block = [block_at(down, place) for place in places]
    line = block[0].astype(jnp.float32)
    for mask in (2, 1, 3):
        line = line + over_y(block[mask], mask).astype(jnp.float32)
    line = line.astype(jnp.bfloat16)
    result = state
    for place in range(4):
        piece = line[place * tokens : (place + 1) * tokens]
        result = result + sent(piece, line_target(place)).astype(jnp.float32)
    return result


def solution(mesh):
    split = Mesh(mesh.devices.reshape(4, 4, 2, 4, 2), ("y", "zl", "zh", "x", "core"))
    all_rows = (*REQ, "core")
    in_specs = (
        P(REQ, None, KVH),
        P(REQ, None, KVH),
        P(REQ, None, KVH),
        P(REQ, KVH, "core", None),
        P(REQ, KVH, "core", None),
        P(),
        P(REQ, None),
        P(all_rows, KVH),
        P(KVH, all_rows),
        P(KVH),
        P(KVH, all_rows),
        P(KVH, all_rows),
        P(all_rows, KVH),
    )
    return jax.shard_map(
        local, mesh=split, in_specs=in_specs, out_specs=P(all_rows, KVH), check_vma=False
    )
```
